256 devices in a mesh: freq: 4 (over x), row: 32 (over z, y), col: 2 (over core).
Axes of the slice: x: 4, y: 4, z: 8, core: 2. Of those that a mesh axis runs over, the one named last changes fastest.
Arguments:
- spectra: bfloat16 [2048, 4, 128, 128], P(('row', 'col'), 'freq'), may hold values from -56 to 56
- basis: bfloat16 [128, 64], replicated, may hold values from -0.5 to 0.5
- start_vectors: bfloat16 [8192, 8, 128], P(('row', 'col'), 'freq'), may hold values from -128 to 128
- pattern: int32 [64, 32, 2, 1], P('row', None, 'col'), may hold values from 0 to 1, as said below
Outputs:
- vectors: bfloat16 [8192, 8, 128], P(('row', 'col'), 'freq')
- affinity: float32 [64, 32, 2, 1, 128, 128], P('row', None, 'col', None, 'freq')
The draws below stay inside these ranges and needn't reach their ends.
Inputs may be any that keep to these rules, and one draw needn't show every extreme that they name: `pattern`: every block is kept with itself. In each block row at most 12 blocks of each column set c are kept; every block row of one group of 2 consecutive block rows keeps exactly 12 in every column set, so the tile of block rows r * 2 to r * 2 + 1 and column set c holds at most 24 kept blocks, and some tile holds exactly 24.
All inputs are finite; a program needn't handle non-finite values.
Results may differ from the reference program's by a relative error of at most 0.015.
Values may be sent and summed in bfloat16 or wider, within the bound.
No kernel may reach another device: no remote copies, remote signals or barrier semaphores. Data moves between devices by JAX's collectives and lax.ppermute only.
A program may use at most 64 MiB of HBM per device.

```python
import math
import jax
import jax.numpy as jnp
from jax import lax

ANG = 128
RAD = 128
COMP = 64
COLS = 64
BLK = 128
ITERS = 2
GROUPS = 4
FREQS = 8
IMAGES = 8192
SEGB = 1
NB = 64
ROWG = 32
COLG = 2
TROWS = 2
TCOLS = 32
WMAX = 12


def draw_spectra(key, part):
    image_key, noise_key = jax.random.split(jax.random.fold_in(key, 11), 2)
    full_shape = (IMAGES // GROUPS, GROUPS, ANG, RAD)
    noise = jax.random.truncated_normal(noise_key, -4.0, 4.0, full_shape, jnp.float32)
    scales = jnp.exp(jax.random.uniform(image_key, (IMAGES // GROUPS, GROUPS, 1, 1), jnp.float32, 0.0, jnp.log(3.0)))
    values = scales * noise
    return values.astype(jnp.bfloat16)


def draw_start_vectors(key, part):
    noise_key, image_key, column_key = jax.random.split(jax.random.fold_in(key, 37), 3)
    full_shape = (IMAGES, FREQS, 2 * COLS)
    position = jnp.arange(IMAGES, dtype=jnp.float32) / IMAGES
    noise = jax.random.truncated_normal(noise_key, -6.0, 6.0, full_shape, jnp.float32)
    image_scale = jnp.exp(jax.random.uniform(image_key, (IMAGES, 1, 1), jnp.float32, 0.0, 0.5 * jnp.log(10.0)))
    column_half = jnp.exp(jax.random.uniform(column_key, (1, FREQS, COLS), jnp.float32, 0.0, 0.5 * jnp.log(10.0)))
    rise = jnp.exp(position * 0.5 * jnp.log(3.0))[:, None, None]
    values = rise * image_scale * jnp.concatenate([column_half, column_half], axis=-1) * noise
    return values.astype(jnp.bfloat16)


def draw_pattern(key, part):
    score_key, weight_key, heavy_key = jax.random.split(jax.random.fold_in(key, 23), 3)
    block_ids = jnp.arange(NB, dtype=jnp.int32)
    heavy_group = jax.random.randint(heavy_key, (), 0, ROWG)
    drawn_weight = jax.random.randint(weight_key, (NB,), 1, WMAX + 1)
    row_weight = jnp.where(block_ids // TROWS == heavy_group, WMAX, drawn_weight)
    scores = jax.random.randint(score_key, (NB, COLG, TCOLS), 0, 1 << 20)
    local_ids = jnp.arange(TCOLS, dtype=jnp.int32)
    scores = scores * TCOLS + local_ids[None, None, :]
    own_segment = block_ids // SEGB
    diag_column = own_segment % COLG
    diag_local = own_segment // COLG * SEGB + block_ids % SEGB
    column_ids = jnp.arange(COLG, dtype=jnp.int32)
    is_diag = (column_ids[None, :, None] == diag_column[:, None, None]) & (local_ids[None, None, :] == diag_local[:, None, None])
    scores = jnp.where(is_diag, 1 << 30, scores)
    ranking = jnp.argsort(jnp.argsort(-scores, axis=2), axis=2)
    kept_flags = (ranking < row_weight[:, None, None]).astype(jnp.int32)
    kept_flags = kept_flags.reshape(NB, COLG, ROWG, SEGB)
    return jnp.transpose(kept_flags, (0, 2, 1, 3))


def scatter_about(rng, dims, spread, reach, kind=jnp.bfloat16):
    entries = spread * jax.random.normal(rng, dims, jnp.float32)
    return jnp.clip(entries, min=-reach, max=reach).astype(kind)


def setup_inputs(seed: int = 0) -> dict:
    streams_of = jax.random.split(jax.random.key(seed), 5)
    spectra = draw_spectra(jax.random.fold_in(streams_of[4], 71), 0)
    basis = scatter_about(streams_of[1], (RAD, COMP), RAD ** -0.5, 0.5)
    start_vectors = draw_start_vectors(jax.random.fold_in(streams_of[4], 71), 0)
    pattern = draw_pattern(jax.random.fold_in(streams_of[4], 71), 0)
    return {"spectra": spectra, "basis": basis, "start_vectors": start_vectors, "pattern": pattern}


def make_table(angles, freq_count):
    angle_ids = jnp.arange(angles, dtype=jnp.int32)
    orders = jnp.arange(freq_count, dtype=jnp.int32) + 1
    phase_steps = angle_ids[:, None] * orders[None, :] % angles
    phase_angle = phase_steps.astype(jnp.float32) * (2.0 * math.pi / angles)
    table_scale = 1.0 / math.sqrt(angles)
    return jnp.stack([jnp.cos(phase_angle) * table_scale, -jnp.sin(phase_angle) * table_scale], axis=1).astype(jnp.bfloat16)

def rounded_copy(values):
    return lax.optimization_barrier(values.astype(jnp.bfloat16)).astype(jnp.float32)

def cross_blocks(left_rows, right_rows):
    half_len = left_rows.shape[-1] // 2
    real_part = jnp.einsum('ufm,rvfm->rfuv', left_rows, right_rows)
    swapped = jnp.concatenate([-right_rows[..., half_len:], right_rows[..., :half_len]], axis=-1)
    imag_part = jnp.einsum('ufm,rvfm->rfuv', left_rows, swapped)
    return (real_part, imag_part)

def reference(spectra, basis, start_vectors, pattern):
    dft_table = make_table(ANG, FREQS).astype(jnp.float32)
    angular = lax.dot_general(dft_table, spectra.astype(jnp.float32), (((0,), (2,)), ((), ()))).astype(jnp.bfloat16)
    radial = lax.dot_general(angular.astype(jnp.float32), basis.astype(jnp.float32), (((4,), (0,)), ((), ()))).astype(jnp.bfloat16)
    coefs = jnp.transpose(radial, (2, 3, 1, 0, 4)).reshape(IMAGES, FREQS, 2 * COMP)
    full_mask = pattern.reshape(NB, NB)
    row_most = WMAX * COLG
    kept_cols = jnp.argsort(1 - full_mask, axis=1, stable=True)[:, :row_most].astype(jnp.int32)
    kept_live = jnp.take_along_axis(full_mask, kept_cols, axis=1).astype(jnp.float32)
    coef_blocks = coefs.reshape(NB, BLK, FREQS, 2 * COMP).astype(jnp.float32)

    def sweep(vectors):
        vector_blocks = vectors.reshape(NB, BLK, FREQS, 2 * COLS).astype(jnp.float32)

        def row_pass(block_idx):
            cols_here = kept_cols[block_idx]
            live_here = kept_live[block_idx][:, None, None, None]
            cross_re, cross_im = cross_blocks(coef_blocks[block_idx], coef_blocks[cols_here])
            cross_re = cross_re / COMP
            cross_im = cross_im / COMP
            kernel_re = rounded_copy((cross_re * cross_re - cross_im * cross_im) * live_here)
            kernel_im = rounded_copy(2.0 * cross_re * cross_im * live_here)
            magnitude = cross_re * cross_re + cross_im * cross_im
            power_rows = lax.optimization_barrier(jnp.sum(magnitude * magnitude * live_here, axis=(0, 3)))
            right_vectors = vector_blocks[cols_here]
            right_re = right_vectors[..., :COLS]
            right_im = right_vectors[..., COLS:]
            result_re = jnp.einsum('rfuv,rvfl->ufl', kernel_re, right_re) - jnp.einsum('rfuv,rvfl->ufl', kernel_im, right_im)
            result_im = jnp.einsum('rfuv,rvfl->ufl', kernel_re, right_im) + jnp.einsum('rfuv,rvfl->ufl', kernel_im, right_re)
            return (jnp.concatenate([result_re, result_im], axis=-1), power_rows.T)
        rows_out, powers = lax.map(row_pass, jnp.arange(NB, dtype=jnp.int32))
        return (rows_out.reshape(IMAGES, FREQS, 2 * COLS), powers.reshape(IMAGES, FREQS))
    vectors = start_vectors
    for step_idx in range(ITERS):
        summed, power_total = sweep(vectors)
        degree = jnp.sqrt(power_total)
        scaled = summed / degree[..., None]
        mean_square = lax.optimization_barrier(jnp.mean(scaled[..., :COLS] * scaled[..., :COLS] + scaled[..., COLS:] * scaled[..., COLS:], axis=0))
        factor = lax.rsqrt(mean_square + 1e-06)
        vectors = (scaled * jnp.concatenate([factor, factor], axis=-1)[None]).astype(jnp.bfloat16)
    final_blocks = vectors.reshape(NB, BLK, FREQS, 2 * COLS).astype(jnp.float32)

    def affinity_row(block_idx):
        cols_here = kept_cols[block_idx]
        gram_re, gram_im = cross_blocks(final_blocks[block_idx], final_blocks[cols_here])
        values = lax.optimization_barrier(jnp.sum(gram_re * gram_re + gram_im * gram_im, axis=1))
        values = values * (kept_live[block_idx][:, None, None] / (COLS * FREQS))
        return jnp.zeros((NB, BLK, BLK), jnp.float32).at[cols_here].set(values)
    affinity = lax.map(affinity_row, jnp.arange(NB, dtype=jnp.int32))
    return (vectors, affinity.reshape(NB, ROWG, COLG, SEGB, BLK, BLK))
```

```python
import math

import jax
import jax.numpy as jnp
from jax import lax
from jax.experimental import pallas as pl
from jax.experimental.pallas import tpu as pltpu
from jax.sharding import Mesh
from jax.sharding import PartitionSpec as P

ANG = 128
COMP = 64
COLS = 64
BLK = 128
FREQ_DEV = 2
IMG_DEV = 32
Z = 8
YC = 8
EXTRA = 16
MSG = FREQ_DEV * BLK + EXTRA
SPAN = Z * BLK
ROW = ("row_0", "row_1")
ROW_COL = ("row_0", "row_1", "col")
YCOL = ("row_1", "col")
F32 = jnp.float32
BF16 = jnp.bfloat16


def make_table(angles, freq_count):
    angle_ids = jnp.arange(angles, dtype=jnp.int32)
    orders = jnp.arange(freq_count, dtype=jnp.int32) + 1
    phase_steps = angle_ids[:, None] * orders[None, :] % angles
    phase_angle = phase_steps.astype(jnp.float32) * (2.0 * math.pi / angles)
    table_scale = 1.0 / math.sqrt(angles)
    return jnp.stack(
        [jnp.cos(phase_angle) * table_scale, -jnp.sin(phase_angle) * table_scale], axis=1
    ).astype(jnp.bfloat16)


def nt_dot(left, right):
    return lax.dot_general(
        left, right, (((1,), (1,)), ((), ())), preferred_element_type=jnp.float32
    )


def lane_signs(shape):
    lanes = lax.broadcasted_iota(jnp.int32, shape, len(shape) - 1)
    return jnp.where(lanes < COMP, -1.0, 1.0).astype(F32)


def swapped(block):
    wide = block.astype(F32)
    return (pltpu.roll(wide, COMP, 1) * lane_signs(wide.shape)).astype(BF16)


def swapped_back(block):
    wide = block.astype(F32)
    return (pltpu.roll(wide, COMP, 1) * -lane_signs(wide.shape)).astype(BF16)


def split_rows(rows):
    high = rows.astype(BF16)
    low = (rows - high.astype(F32)).astype(BF16)
    zeros = jnp.zeros((EXTRA - 4, BLK), BF16)
    return jnp.concatenate([high.astype(F32), low.astype(F32), zeros.astype(F32)], axis=0).astype(
        BF16
    )


def joined_rows(extra):
    total = jnp.sum(extra.astype(F32), axis=0)
    return total[0:2] + total[2:4]


def to_column(row):
    rows = lax.broadcasted_iota(jnp.int32, (BLK, BLK), 0)
    cols = lax.broadcasted_iota(jnp.int32, (BLK, BLK), 1)
    return jnp.sum(jnp.where(rows == cols, row, 0.0), axis=1, keepdims=True)


def load_stack(stack_ref, vec_ref, offset):
    for f in range(FREQ_DEV):
        for z in range(Z):
            block = vec_ref[z, offset + f * BLK : offset + (f + 1) * BLK, :]
            stack_ref[f, z * BLK : (z + 1) * BLK, :] = block
            stack_ref[f, SPAN + z * BLK : SPAN + (z + 1) * BLK, :] = swapped(block)


def mask_rows(mask_ref, which):
    extra = mask_ref[0].astype(F32)
    return jnp.where(which % 2 == 0, extra[0:Z], extra[Z : 2 * Z])


def cross_kernel(col_id, rows_ref, mask_ref, cols_ref, kern_ref, msg_ref, stack_ref):
    step = pl.program_id(0)

    @pl.when(step == 0)
    def _():
        load_stack(stack_ref, cols_ref, FREQ_DEV * BLK)

    masks = mask_rows(mask_ref, step)
    powers = []
    for f in range(FREQ_DEV):
        block = rows_ref[0, f * BLK : (f + 1) * BLK, :] * jnp.asarray(1.0 / COMP, BF16)
        left = jnp.concatenate([block, swapped_back(block)], axis=0)
        acc = jnp.zeros((BLK, BLK), F32)
        for z in range(Z):
            cross = nt_dot(left, cols_ref[z, f * BLK : (f + 1) * BLK, :])
            mask = masks[z : z + 1, :]
            re = cross[:BLK] * mask
            im = cross[BLK:] * mask
            re2 = re * re
            im2 = im * im
            kern_ref[0, f, :, z * BLK : (z + 1) * BLK] = (re2 - im2).astype(BF16)
            kern_ref[0, f, :, SPAN + z * BLK : SPAN + (z + 1) * BLK] = (2.0 * re * im).astype(BF16)
            mag = re2 + im2
            acc = acc + mag * mag
        high = acc.astype(BF16)
        low = (acc - high.astype(F32)).astype(BF16)
        ones = jnp.ones((EXTRA, BLK), BF16)
        powers.append((nt_dot(ones, high) + nt_dot(ones, low))[0:1])
        product = jnp.dot(kern_ref[0, f], stack_ref[f], preferred_element_type=F32)
        msg_ref[0, f * BLK : (f + 1) * BLK, :] = product.astype(BF16)
    msg_ref[0, FREQ_DEV * BLK :, :] = split_rows(jnp.concatenate(powers, axis=0))


def product_kernel(kern_ref, cols_ref, msg_ref, stack_ref, sums_ref):
    step = pl.program_id(0)

    @pl.when(step == 0)
    def _():
        load_stack(stack_ref, cols_ref, 0)
        sums_ref[...] = split_rows(group_sums(cols_ref))

    for f in range(FREQ_DEV):
        product = jnp.dot(kern_ref[0, f], stack_ref[f], preferred_element_type=F32)
        msg_ref[0, f * BLK : (f + 1) * BLK, :] = product.astype(BF16)
    msg_ref[0, FREQ_DEV * BLK :, :] = sums_ref[...]


def group_sums(cols_ref):
    rows = []
    for f in range(FREQ_DEV):
        acc = jnp.zeros((BLK, BLK), F32)
        for z in range(Z):
            block = cols_ref[z, f * BLK : (f + 1) * BLK, :].astype(F32)
            acc = acc + block * block
        rows.append(jnp.sum(acc, axis=0, keepdims=True))
    both = jnp.concatenate(rows + rows + rows + rows, axis=0)
    return (both + pltpu.roll(both, COLS, 1))[0:2]


def first_combine(recv_ref, out_ref, inverse_ref):
    powers = joined_rows(recv_ref[:, FREQ_DEV * BLK :, :])
    inverse = lax.rsqrt(powers)
    for f in range(FREQ_DEV):
        total = jnp.sum(recv_ref[:, f * BLK : (f + 1) * BLK, :].astype(F32), axis=0)
        column = jnp.broadcast_to(to_column(inverse[f : f + 1]), (BLK, BLK))
        inverse_ref[f * BLK : (f + 1) * BLK, :] = column
        value = (total * column).astype(BF16)
        for z in range(Z):
            out_ref[z, f * BLK : (f + 1) * BLK, :] = value


def second_combine(recv_ref, inverse_ref, scaled_ref, out_ref, *, images):
    means = joined_rows(recv_ref[:, FREQ_DEV * BLK :, :]) / images
    factor = lax.rsqrt(means + 1e-06)
    for f in range(FREQ_DEV):
        total = jnp.sum(recv_ref[:, f * BLK : (f + 1) * BLK, :].astype(F32), axis=0)
        value = total * inverse_ref[f * BLK : (f + 1) * BLK, :] * factor[f : f + 1]
        scaled_ref[f * BLK : (f + 1) * BLK, :] = value
        value = value.astype(BF16)
        for z in range(Z):
            out_ref[z, f * BLK : (f + 1) * BLK, :] = value


def sums_message(cols_ref, scaled_ref, out_ref):
    extra = split_rows(group_sums(cols_ref))
    value = scaled_ref[...].astype(BF16)
    for k in range(YC):
        out_ref[k, : FREQ_DEV * BLK, :] = value
        out_ref[k, FREQ_DEV * BLK :, :] = extra


def gram_kernel(
    col_id, rows_ref, mask_ref, sums_ref, cols_ref, scaled_ref, out_ref, vec_ref, *, images, freqs
):
    step = pl.program_id(0)
    means = joined_rows(sums_ref[...]) / images
    factor = lax.rsqrt(means + 1e-06)
    square = factor * factor

    @pl.when(step == 0)
    def _():
        for f in range(FREQ_DEV):
            vec_ref[f] = (scaled_ref[f * BLK : (f + 1) * BLK, :] * factor[f : f + 1]).astype(BF16)

    masks = mask_rows(mask_ref, step) * (1.0 / (COLS * freqs))
    lefts = []
    for f in range(FREQ_DEV):
        block = (rows_ref[0, f * BLK : (f + 1) * BLK, :].astype(F32) * square[f : f + 1]).astype(
            BF16
        )
        lefts.append(jnp.concatenate([block, swapped_back(block)], axis=0))
    for z in range(Z):
        total = jnp.zeros((BLK, BLK), F32)
        for f in range(FREQ_DEV):
            gram = nt_dot(lefts[f], cols_ref[z, f * BLK : (f + 1) * BLK, :])
            total = total + gram[:BLK] * gram[:BLK] + gram[BLK:] * gram[BLK:]
        value = (total * masks[z : z + 1, :]).astype(BF16)
        for x in range(4):
            out_ref[x, 0, z] = value[x * 32 : (x + 1) * 32]


def whole(shape):
    return pl.BlockSpec(shape, lambda *_: (0,) * len(shape))


def exchange(pieces, axes):
    return lax.all_to_all(pieces, axes, 0, 0, tiled=True)


def body(spectra, basis, start_vectors, pattern):
    group_devices = lax.axis_size("freq")
    images = BLK * lax.axis_size(ROW_COL)
    freq_total = FREQ_DEV * group_devices
    col_id = lax.axis_index("col").astype(jnp.int32).reshape(1)
    dft_table = make_table(ANG, freq_total)
    angular = lax.dot_general(
        dft_table, spectra[:, 0], (((0,), (1,)), ((), ())), preferred_element_type=jnp.float32
    ).astype(jnp.bfloat16)
    radial = lax.dot_general(
        angular, basis, (((3,), (0,)), ((), ())), preferred_element_type=jnp.float32
    ).astype(jnp.bfloat16)
    coef_local = jnp.transpose(radial, (1, 2, 0, 3)).reshape(
        group_devices, FREQ_DEV, IMG_DEV, 2 * COMP
    )
    regrouped = exchange(coef_local, "freq")
    own = jnp.transpose(regrouped, (1, 2, 0, 3)).reshape(FREQ_DEV * BLK, 2 * COMP)
    start = jnp.transpose(start_vectors, (1, 0, 2)).reshape(FREQ_DEV * BLK, 2 * COLS)
    to_z = jnp.concatenate([own, start], axis=0)
    cols = exchange(jnp.broadcast_to(to_z, (Z, *to_z.shape)), "row_0")
    kept = jnp.transpose(pattern.reshape(2, Z, YC // 2), (2, 0, 1)).reshape(YC // 2, 1, EXTRA, 1)
    kept = jnp.broadcast_to(kept.astype(BF16), (YC // 2, 2, EXTRA, BLK)).reshape(YC, EXTRA, BLK)
    to_yc = jnp.concatenate([jnp.broadcast_to(own, (YC, *own.shape)), kept], axis=1)
    rows = exchange(to_yc, YCOL)

    row_spec = pl.BlockSpec((1, FREQ_DEV * BLK, BLK), lambda i, c: (i, 0, 0))
    mask_spec = pl.BlockSpec((1, EXTRA, BLK), lambda i, c: (i // 2 * 2 + c[0], 16, 0))
    big = pltpu.CompilerParams(vmem_limit_bytes=48 << 20)
    stack = pltpu.VMEM((FREQ_DEV, 2 * SPAN, BLK), BF16)
    msg_shape = jax.ShapeDtypeStruct((YC, MSG, BLK), BF16)
    kernels, partial = pl.pallas_call(
        cross_kernel,
        grid_spec=pltpu.PrefetchScalarGridSpec(
            num_scalar_prefetch=1,
            grid=(YC,),
            in_specs=[row_spec, mask_spec, whole(cols.shape)],
            out_specs=[
                pl.BlockSpec((1, FREQ_DEV, BLK, 2 * SPAN), lambda i, c: (i, 0, 0, 0)),
                pl.BlockSpec((1, MSG, BLK), lambda i, c: (i, 0, 0)),
            ],
            scratch_shapes=[stack],
        ),
        out_shape=[jax.ShapeDtypeStruct((YC, FREQ_DEV, BLK, 2 * SPAN), BF16), msg_shape],
        compiler_params=big,
        name="cross",
    )(col_id, rows, rows, cols)
    got = exchange(partial, YCOL)
    own_shape = (FREQ_DEV * BLK, BLK)
    to_z, inverse = pl.pallas_call(
        first_combine,
        out_shape=[
            jax.ShapeDtypeStruct((Z, *own_shape), BF16),
            jax.ShapeDtypeStruct(own_shape, F32),
        ],
        name="combine_one",
    )(got)
    cols = exchange(to_z, "row_0")
    partial = pl.pallas_call(
        product_kernel,
        grid=(YC,),
        in_specs=[
            pl.BlockSpec((1, FREQ_DEV, BLK, 2 * SPAN), lambda i: (i, 0, 0, 0)),
            whole(cols.shape),
        ],
        out_specs=pl.BlockSpec((1, MSG, BLK), lambda i: (i, 0, 0)),
        out_shape=msg_shape,
        scratch_shapes=[stack, pltpu.VMEM((EXTRA, BLK), BF16)],
        compiler_params=big,
        name="product",
    )(kernels, cols)
    got = exchange(partial, YCOL)
    scaled, to_z = pl.pallas_call(
        lambda *refs: second_combine(*refs, images=images),
        out_shape=[
            jax.ShapeDtypeStruct(own_shape, F32),
            jax.ShapeDtypeStruct((Z, *own_shape), BF16),
        ],
        name="combine_two",
    )(got, inverse)
    cols = exchange(to_z, "row_0")
    to_yc = pl.pallas_call(sums_message, out_shape=msg_shape, name="sums")(cols, scaled)
    last_rows = exchange(to_yc, YCOL)
    tiles, vectors = pl.pallas_call(
        lambda *refs: gram_kernel(*refs, images=images, freqs=freq_total),
        grid_spec=pltpu.PrefetchScalarGridSpec(
            num_scalar_prefetch=1,
            grid=(YC,),
            in_specs=[
                row_spec,
                mask_spec,
                pl.BlockSpec((YC, EXTRA, BLK), lambda i, c: (0, 16, 0)),
                whole(cols.shape),
                whole(own_shape),
            ],
            out_specs=[
                pl.BlockSpec((4, 1, Z, 32, BLK), lambda i, c: (0, i, 0, 0, 0)),
                whole((FREQ_DEV, BLK, BLK)),
            ],
        ),
        out_shape=[
            jax.ShapeDtypeStruct((4, YC, Z, 32, BLK), BF16),
            jax.ShapeDtypeStruct((FREQ_DEV, BLK, BLK), BF16),
        ],
        compiler_params=big,
        name="gram",
    )(col_id, last_rows, rows, last_rows, cols, scaled)
    vectors = jnp.transpose(vectors, (1, 0, 2))
    arrived = exchange(tiles.reshape(16, 2, Z, 32, BLK), ("freq", "row_1"))
    summed = jnp.sum(arrived.reshape(4, 4, 2, Z, 32, BLK).astype(F32), axis=0)
    affinity = jnp.transpose(summed, (1, 2, 0, 3, 4)).reshape(2, 32, 1, 1, 32, BLK)
    return (vectors, affinity)


def solution(mesh):
    split = Mesh(
        mesh.devices.reshape(mesh.shape["freq"], 8, 4, mesh.shape["col"]),
        ("freq", "row_0", "row_1", "col"),
    )
    placed = (
        P(ROW_COL, "freq", None, None),
        P(),
        P(ROW_COL, "freq", None),
        P(ROW, None, "col", None),
    )
    return jax.shard_map(
        body,
        mesh=split,
        in_specs=placed,
        out_specs=(P(ROW_COL, "freq", None), P(ROW, None, "col", None, "freq", None)),
        check_vma=False,
    )
```

```python
import math

import jax
import jax.numpy as jnp
from jax import lax
from jax.experimental import pallas as pl
from jax.experimental.pallas import tpu as pltpu
from jax.sharding import Mesh
from jax.sharding import PartitionSpec as P

ANG = 128
COMP = 64
COLS = 64
BLK = 128
FREQ_DEV = 2
IMG_DEV = 32
Z = 8
YC = 8
EXTRA = 16
MSG = FREQ_DEV * BLK + EXTRA
SPAN = Z * BLK
ROW = ("row_0", "row_1")
ROW_COL = ("row_0", "row_1", "col")
YCOL = ("row_1", "col")
F32 = jnp.float32
BF16 = jnp.bfloat16


def make_table(angles, freq_count):
    angle_ids = jnp.arange(angles, dtype=jnp.int32)
    orders = jnp.arange(freq_count, dtype=jnp.int32) + 1
    phase_steps = angle_ids[:, None] * orders[None, :] % angles
    phase_angle = phase_steps.astype(jnp.float32) * (2.0 * math.pi / angles)
    table_scale = 1.0 / math.sqrt(angles)
    return jnp.stack(
        [jnp.cos(phase_angle) * table_scale, -jnp.sin(phase_angle) * table_scale], axis=1
    ).astype(jnp.bfloat16)


def nt_dot(left, right):
    return lax.dot_general(
        left, right, (((1,), (1,)), ((), ())), preferred_element_type=jnp.float32
    )


def lane_signs(shape):
    lanes = lax.broadcasted_iota(jnp.int32, shape, len(shape) - 1)
    return jnp.where(lanes < COMP, -1.0, 1.0).astype(F32)


def swapped(block):
    wide = block.astype(F32)
    return (pltpu.roll(wide, COMP, 1) * lane_signs(wide.shape)).astype(BF16)


def swapped_back(block):
    wide = block.astype(F32)
    return (pltpu.roll(wide, COMP, 1) * -lane_signs(wide.shape)).astype(BF16)


def split_rows(rows):
    high = rows.astype(BF16)
    low = (rows - high.astype(F32)).astype(BF16)
    zeros = jnp.zeros((EXTRA - 4, BLK), BF16)
    return jnp.concatenate([high.astype(F32), low.astype(F32), zeros.astype(F32)], axis=0).astype(
        BF16
    )


def joined_rows(extra):
    total = jnp.sum(extra.astype(F32), axis=0)
    return total[0:2] + total[2:4]


def to_column(row):
    rows = lax.broadcasted_iota(jnp.int32, (BLK, BLK), 0)
    cols = lax.broadcasted_iota(jnp.int32, (BLK, BLK), 1)
    return jnp.sum(jnp.where(rows == cols, row, 0.0), axis=1, keepdims=True)


def load_stack(stack_ref, vec_ref, offset):
    for f in range(FREQ_DEV):
        for z in range(Z):
            block = vec_ref[z, offset + f * BLK : offset + (f + 1) * BLK, :]
            stack_ref[f, z * BLK : (z + 1) * BLK, :] = block
            stack_ref[f, SPAN + z * BLK : SPAN + (z + 1) * BLK, :] = swapped(block)


def mask_rows(mask_ref, which):
    extra = mask_ref[0].astype(F32)
    return jnp.where(which % 2 == 0, extra[0:Z], extra[Z : 2 * Z])


def cross_kernel(col_id, rows_ref, mask_ref, cols_ref, kern_ref, msg_ref, stack_ref):
    step = pl.program_id(0)

    @pl.when(step == 0)
    def _():
        load_stack(stack_ref, cols_ref, FREQ_DEV * BLK)

    masks = mask_rows(mask_ref, step)
    powers = []
    for f in range(FREQ_DEV):
        block = rows_ref[0, f * BLK : (f + 1) * BLK, :] * jnp.asarray(1.0 / COMP, BF16)
        left = jnp.concatenate([block, swapped_back(block)], axis=0)
        acc = jnp.zeros((BLK, BLK), F32)
        for z in range(Z):
            cross = nt_dot(left, cols_ref[z, f * BLK : (f + 1) * BLK, :])
            mask = masks[z : z + 1, :]
            re = cross[:BLK] * mask
            im = cross[BLK:] * mask
            re2 = re * re
            im2 = im * im
            kern_ref[0, f, :, z * BLK : (z + 1) * BLK] = (re2 - im2).astype(BF16)
            kern_ref[0, f, :, SPAN + z * BLK : SPAN + (z + 1) * BLK] = (2.0 * re * im).astype(BF16)
            mag = re2 + im2
            acc = acc + mag * mag
        high = acc.astype(BF16)
        low = (acc - high.astype(F32)).astype(BF16)
        ones = jnp.ones((EXTRA, BLK), BF16)
        powers.append((nt_dot(ones, high) + nt_dot(ones, low))[0:1])
        product = jnp.dot(kern_ref[0, f], stack_ref[f], preferred_element_type=F32)
        msg_ref[0, f * BLK : (f + 1) * BLK, :] = product.astype(BF16)
    msg_ref[0, FREQ_DEV * BLK :, :] = split_rows(jnp.concatenate(powers, axis=0))


def product_kernel(kern_ref, cols_ref, msg_ref, stack_ref, sums_ref):
    step = pl.program_id(0)

    @pl.when(step == 0)
    def _():
        load_stack(stack_ref, cols_ref, 0)
        sums_ref[...] = split_rows(group_sums(cols_ref))

    for f in range(FREQ_DEV):
        product = jnp.dot(kern_ref[0, f], stack_ref[f], preferred_element_type=F32)
        msg_ref[0, f * BLK : (f + 1) * BLK, :] = product.astype(BF16)
    msg_ref[0, FREQ_DEV * BLK :, :] = sums_ref[...]


def group_sums(cols_ref):
    rows = []
    for f in range(FREQ_DEV):
        acc = jnp.zeros((BLK, BLK), F32)
        for z in range(Z):
            block = cols_ref[z, f * BLK : (f + 1) * BLK, :].astype(F32)
            acc = acc + block * block
        rows.append(jnp.sum(acc, axis=0, keepdims=True))
    both = jnp.concatenate(rows + rows + rows + rows, axis=0)
    return (both + pltpu.roll(both, COLS, 1))[0:2]


def first_combine(recv_ref, out_ref, inverse_ref):
    powers = joined_rows(recv_ref[:, FREQ_DEV * BLK :, :])
    inverse = lax.rsqrt(powers)
    for f in range(FREQ_DEV):
        total = jnp.sum(recv_ref[:, f * BLK : (f + 1) * BLK, :].astype(F32), axis=0)
        column = jnp.broadcast_to(to_column(inverse[f : f + 1]), (BLK, BLK))
        inverse_ref[f * BLK : (f + 1) * BLK, :] = column
        value = (total * column).astype(BF16)
        for z in range(Z):
            out_ref[z, f * BLK : (f + 1) * BLK, :] = value


def second_combine(recv_ref, inverse_ref, scaled_ref, out_ref, *, images):
    means = joined_rows(recv_ref[:, FREQ_DEV * BLK :, :]) / images
    factor = lax.rsqrt(means + 1e-06)
    for f in range(FREQ_DEV):
        total = jnp.sum(recv_ref[:, f * BLK : (f + 1) * BLK, :].astype(F32), axis=0)
        value = total * inverse_ref[f * BLK : (f + 1) * BLK, :] * factor[f : f + 1]
        scaled_ref[f * BLK : (f + 1) * BLK, :] = value
        value = value.astype(BF16)
        for z in range(Z):
            out_ref[z, f * BLK : (f + 1) * BLK, :] = value


def sums_message(cols_ref, scaled_ref, out_ref):
    extra = split_rows(group_sums(cols_ref))
    value = scaled_ref[...].astype(BF16)
    for k in range(YC):
        out_ref[k, : FREQ_DEV * BLK, :] = value
        out_ref[k, FREQ_DEV * BLK :, :] = extra


def gram_kernel(
    col_id, rows_ref, mask_ref, sums_ref, cols_ref, scaled_ref, out_ref, vec_ref, *, images, freqs
):
    step = pl.program_id(0)
    means = joined_rows(sums_ref[...]) / images
    factor = lax.rsqrt(means + 1e-06)
    square = factor * factor

    @pl.when(step == 0)
    def _():
        for f in range(FREQ_DEV):
            vec_ref[f] = (scaled_ref[f * BLK : (f + 1) * BLK, :] * factor[f : f + 1]).astype(BF16)

    masks = mask_rows(mask_ref, step) * (1.0 / (COLS * freqs))
    lefts = []
    for f in range(FREQ_DEV):
        block = (rows_ref[0, f * BLK : (f + 1) * BLK, :].astype(F32) * square[f : f + 1]).astype(
            BF16
        )
        lefts.append(jnp.concatenate([block, swapped_back(block)], axis=0))
    for z in range(Z):
        total = jnp.zeros((BLK, BLK), F32)
        for f in range(FREQ_DEV):
            gram = nt_dot(lefts[f], cols_ref[z, f * BLK : (f + 1) * BLK, :])
            total = total + gram[:BLK] * gram[:BLK] + gram[BLK:] * gram[BLK:]
        value = (total * masks[z : z + 1, :]).astype(BF16)
        for x in range(4):
            out_ref[x, 0, z] = value[x * 32 : (x + 1) * 32]


def final_sum(tiles_ref, out_ref):
    for y in range(4):
        for z in range(Z // 2):
            total = tiles_ref[0, y, 0, z].astype(F32)
            for x in range(1, 4):
                total = total + tiles_ref[x, y, 0, z].astype(F32)
            out_ref[0, z, y] = total


def whole(shape):
    return pl.BlockSpec(shape, lambda *_: (0,) * len(shape))


def exchange(pieces, axes):
    return lax.all_to_all(pieces, axes, 0, 0, tiled=True)


def body(spectra, basis, start_vectors, pattern):
    group_devices = lax.axis_size("freq")
    images = BLK * lax.axis_size(ROW_COL)
    freq_total = FREQ_DEV * group_devices
    col_id = lax.axis_index("col").astype(jnp.int32).reshape(1)
    dft_table = make_table(ANG, freq_total)
    angular = lax.dot_general(
        dft_table, spectra[:, 0], (((0,), (1,)), ((), ())), preferred_element_type=jnp.float32
    ).astype(jnp.bfloat16)
    radial = lax.dot_general(
        angular, basis, (((3,), (0,)), ((), ())), preferred_element_type=jnp.float32
    ).astype(jnp.bfloat16)
    coef_local = jnp.transpose(radial, (1, 2, 0, 3)).reshape(
        group_devices, FREQ_DEV, IMG_DEV, 2 * COMP
    )
    regrouped = exchange(coef_local, "freq")
    own = jnp.transpose(regrouped, (1, 2, 0, 3)).reshape(FREQ_DEV * BLK, 2 * COMP)
    start = jnp.transpose(start_vectors, (1, 0, 2)).reshape(FREQ_DEV * BLK, 2 * COLS)
    to_z = jnp.concatenate([own, start], axis=0)
    cols = exchange(jnp.broadcast_to(to_z, (Z, *to_z.shape)), "row_0")
    kept = jnp.transpose(pattern.reshape(2, Z, YC // 2), (2, 0, 1)).reshape(YC // 2, 1, EXTRA, 1)
    kept = jnp.broadcast_to(kept.astype(BF16), (YC // 2, 2, EXTRA, BLK)).reshape(YC, EXTRA, BLK)
    to_yc = jnp.concatenate([jnp.broadcast_to(own, (YC, *own.shape)), kept], axis=1)
    rows = exchange(to_yc, YCOL)

    row_spec = pl.BlockSpec((1, FREQ_DEV * BLK, BLK), lambda i, c: (i, 0, 0))
    mask_spec = pl.BlockSpec((1, EXTRA, BLK), lambda i, c: (i // 2 * 2 + c[0], 16, 0))
    big = pltpu.CompilerParams(vmem_limit_bytes=16 << 20)
    small = pltpu.CompilerParams(vmem_limit_bytes=6 << 20)
    stack = pltpu.VMEM((FREQ_DEV, 2 * SPAN, BLK), BF16)
    msg_shape = jax.ShapeDtypeStruct((YC, MSG, BLK), BF16)
    kernels, partial = pl.pallas_call(
        cross_kernel,
        grid_spec=pltpu.PrefetchScalarGridSpec(
            num_scalar_prefetch=1,
            grid=(YC,),
            in_specs=[row_spec, mask_spec, whole(cols.shape)],
            out_specs=[
                pl.BlockSpec((1, FREQ_DEV, BLK, 2 * SPAN), lambda i, c: (i, 0, 0, 0)),
                pl.BlockSpec((1, MSG, BLK), lambda i, c: (i, 0, 0)),
            ],
            scratch_shapes=[stack],
        ),
        out_shape=[jax.ShapeDtypeStruct((YC, FREQ_DEV, BLK, 2 * SPAN), BF16), msg_shape],
        compiler_params=big,
        name="cross",
    )(col_id, rows, rows, cols)
    got = exchange(partial, YCOL)
    own_shape = (FREQ_DEV * BLK, BLK)
    to_z, inverse = pl.pallas_call(
        first_combine,
        out_shape=[
            jax.ShapeDtypeStruct((Z, *own_shape), BF16),
            jax.ShapeDtypeStruct(own_shape, F32),
        ],
        compiler_params=small,
        name="combine_one",
    )(got)
    cols = exchange(to_z, "row_0")
    partial = pl.pallas_call(
        product_kernel,
        grid=(YC,),
        in_specs=[
            pl.BlockSpec((1, FREQ_DEV, BLK, 2 * SPAN), lambda i: (i, 0, 0, 0)),
            whole(cols.shape),
        ],
        out_specs=pl.BlockSpec((1, MSG, BLK), lambda i: (i, 0, 0)),
        out_shape=msg_shape,
        scratch_shapes=[stack, pltpu.VMEM((EXTRA, BLK), BF16)],
        compiler_params=big,
        name="product",
    )(kernels, cols)
    got = exchange(partial, YCOL)
    scaled, to_z = pl.pallas_call(
        lambda *refs: second_combine(*refs, images=images),
        out_shape=[
            jax.ShapeDtypeStruct(own_shape, F32),
            jax.ShapeDtypeStruct((Z, *own_shape), BF16),
        ],
        compiler_params=small,
        name="combine_two",
    )(got, inverse)
    cols = exchange(to_z, "row_0")
    to_yc = pl.pallas_call(
        sums_message, out_shape=msg_shape, compiler_params=small, name="sums"
    )(cols, scaled)
    last_rows = exchange(to_yc, YCOL)
    tiles, vectors = pl.pallas_call(
        lambda *refs: gram_kernel(*refs, images=images, freqs=freq_total),
        grid_spec=pltpu.PrefetchScalarGridSpec(
            num_scalar_prefetch=1,
            grid=(YC,),
            in_specs=[
                row_spec,
                mask_spec,
                pl.BlockSpec((YC, EXTRA, BLK), lambda i, c: (0, 16, 0)),
                whole(cols.shape),
                whole(own_shape),
            ],
            out_specs=[
                pl.BlockSpec((4, 1, Z, 32, BLK), lambda i, c: (0, i, 0, 0, 0)),
                whole((FREQ_DEV, BLK, BLK)),
            ],
        ),
        out_shape=[
            jax.ShapeDtypeStruct((4, YC, Z, 32, BLK), BF16),
            jax.ShapeDtypeStruct((FREQ_DEV, BLK, BLK), BF16),
        ],
        compiler_params=big,
        name="gram",
    )(col_id, last_rows, rows, last_rows, cols, scaled)
    arrived = exchange(tiles.reshape(16, 2, Z, 32, BLK), ("freq", "row_1"))
    arrived, vectors = lax.optimization_barrier((arrived, vectors))
    vectors = jnp.transpose(vectors, (1, 0, 2))
    affinity = pl.pallas_call(
        final_sum,
        grid=(2, 2),
        in_specs=[pl.BlockSpec((4, 4, 1, Z // 2, 32, BLK), lambda t, h: (0, 0, t, h, 0, 0))],
        out_specs=pl.BlockSpec((1, Z // 2, 4, 32, BLK), lambda t, h: (t, h, 0, 0, 0)),
        out_shape=jax.ShapeDtypeStruct((2, Z, 4, 32, BLK), F32),
        compiler_params=small,
        name="final",
    )(arrived.reshape(4, 4, 2, Z, 32, BLK))
    return (vectors, affinity.reshape(2, 32, 1, 1, 32, BLK))


def solution(mesh):
    split = Mesh(
        mesh.devices.reshape(mesh.shape["freq"], 8, 4, mesh.shape["col"]),
        ("freq", "row_0", "row_1", "col"),
    )
    placed = (
        P(ROW_COL, "freq", None, None),
        P(),
        P(ROW_COL, "freq", None),
        P(ROW, None, "col", None),
    )
    return jax.shard_map(
        body,
        mesh=split,
        in_specs=placed,
        out_specs=(P(ROW_COL, "freq", None), P(ROW, None, "col", None, "freq", None)),
        check_vma=False,
    )
```

```python
import math

import jax
import jax.numpy as jnp
from jax import lax
from jax.experimental import pallas as pl
from jax.experimental.pallas import tpu as pltpu
from jax.sharding import Mesh
from jax.sharding import PartitionSpec as P

ANG = 128
COMP = 64
COLS = 64
BLK = 128
FREQ_DEV = 2
IMG_DEV = 32
Z = 8
YC = 8
EXTRA = 16
MSG = FREQ_DEV * BLK + EXTRA
SPAN = Z * BLK
ROW = ("row_0", "row_1")
ROW_COL = ("row_0", "row_1", "col")
YCOL = ("row_1", "col")
F32 = jnp.float32
BF16 = jnp.bfloat16


def make_table(angles, freq_count):
    angle_ids = jnp.arange(angles, dtype=jnp.int32)
    orders = jnp.arange(freq_count, dtype=jnp.int32) + 1
    phase_steps = angle_ids[:, None] * orders[None, :] % angles
    phase_angle = phase_steps.astype(jnp.float32) * (2.0 * math.pi / angles)
    table_scale = 1.0 / math.sqrt(angles)
    return jnp.stack(
        [jnp.cos(phase_angle) * table_scale, -jnp.sin(phase_angle) * table_scale], axis=1
    ).astype(jnp.bfloat16)


def nt_dot(left, right):
    return lax.dot_general(
        left, right, (((1,), (1,)), ((), ())), preferred_element_type=jnp.float32
    )


def lane_signs(shape):
    lanes = lax.broadcasted_iota(jnp.int32, shape, len(shape) - 1)
    return jnp.where(lanes < COMP, -1.0, 1.0).astype(F32)


def swapped(block):
    wide = block.astype(F32)
    return (pltpu.roll(wide, COMP, 1) * lane_signs(wide.shape)).astype(BF16)


def swapped_back(block):
    wide = block.astype(F32)
    return (pltpu.roll(wide, COMP, 1) * -lane_signs(wide.shape)).astype(BF16)


def split_rows(rows):
    high = rows.astype(BF16)
    low = (rows - high.astype(F32)).astype(BF16)
    zeros = jnp.zeros((EXTRA - 4, BLK), BF16)
    return jnp.concatenate([high.astype(F32), low.astype(F32), zeros.astype(F32)], axis=0).astype(
        BF16
    )


def joined_rows(extra):
    total = jnp.sum(extra.astype(F32), axis=0)
    return total[0:2] + total[2:4]


def to_column(row):
    rows = lax.broadcasted_iota(jnp.int32, (BLK, BLK), 0)
    cols = lax.broadcasted_iota(jnp.int32, (BLK, BLK), 1)
    return jnp.sum(jnp.where(rows == cols, row, 0.0), axis=1, keepdims=True)


def load_stack(stack_ref, col_refs):
    for f in range(FREQ_DEV):
        for z in range(Z):
            block = col_refs[z][f * BLK : (f + 1) * BLK, :]
            stack_ref[f, z * BLK : (z + 1) * BLK, :] = block
            stack_ref[f, SPAN + z * BLK : SPAN + (z + 1) * BLK, :] = swapped(block)


def prepare(coef_ref, kept_ref, own_ref, msg_ref, wide_ref):
    for q in range(4):
        for f in range(FREQ_DEV):
            wide_ref[pl.ds(f * BLK + q, IMG_DEV, stride=4), :] = coef_ref[q, f].astype(F32)
    own = wide_ref[...].astype(BF16)
    own_ref[...] = own
    for k in range(YC):
        msg_ref[k, : FREQ_DEV * BLK, :] = own
        msg_ref[k, FREQ_DEV * BLK :, :] = kept_ref[k]


def load_masks(mask_ref, scratch_ref, which):
    extra = mask_ref[0].astype(F32)
    scratch_ref[...] = jnp.where(which % 2 == 0, extra[0:Z], extra[Z : 2 * Z])


def cross_kernel(place, rows_ref, mask_ref, *refs):
    col_refs, first_refs = refs[:Z], refs[Z : 2 * Z]
    kern_ref, msg_ref, stack_ref, mask_rows = refs[2 * Z :]
    step = pl.program_id(0)

    @pl.when(step == 0)
    def _():
        load_stack(stack_ref, first_refs)

    load_masks(mask_ref, mask_rows, step)
    powers = []
    for f in range(FREQ_DEV):
        block = rows_ref[0, f * BLK : (f + 1) * BLK, :] * jnp.asarray(1.0 / COMP, BF16)
        left = jnp.concatenate([block, swapped_back(block)], axis=0)
        acc = jnp.zeros((BLK, BLK), F32)
        for z in range(Z):
            cross = nt_dot(left, col_refs[z][f * BLK : (f + 1) * BLK, :])
            mask = mask_rows[pl.ds((place[1] - z) & (Z - 1), 1), :]
            re = cross[:BLK] * mask
            im = cross[BLK:] * mask
            re2 = re * re
            im2 = im * im
            kern_ref[0, f, :, z * BLK : (z + 1) * BLK] = (re2 - im2).astype(BF16)
            kern_ref[0, f, :, SPAN + z * BLK : SPAN + (z + 1) * BLK] = (2.0 * re * im).astype(BF16)
            mag = re2 + im2
            acc = acc + mag * mag
        high = acc.astype(BF16)
        low = (acc - high.astype(F32)).astype(BF16)
        ones = jnp.ones((EXTRA, BLK), BF16)
        powers.append((nt_dot(ones, high) + nt_dot(ones, low))[0:1])
        product = jnp.dot(kern_ref[0, f], stack_ref[f], preferred_element_type=F32)
        msg_ref[0, f * BLK : (f + 1) * BLK, :] = product.astype(BF16)
    msg_ref[0, FREQ_DEV * BLK :, :] = split_rows(jnp.concatenate(powers, axis=0))


def product_kernel(kern_ref, *refs):
    col_refs = refs[:Z]
    msg_ref, stack_ref, sums_ref = refs[Z:]
    step = pl.program_id(0)

    @pl.when(step == 0)
    def _():
        load_stack(stack_ref, col_refs)
        sums_ref[...] = split_rows(block_sums([ref[...].astype(F32) for ref in col_refs]))

    for f in range(FREQ_DEV):
        product = jnp.dot(kern_ref[0, f], stack_ref[f], preferred_element_type=F32)
        msg_ref[0, f * BLK : (f + 1) * BLK, :] = product.astype(BF16)
    msg_ref[0, FREQ_DEV * BLK :, :] = sums_ref[...]


def block_sums(blocks):
    rows = []
    for f in range(FREQ_DEV):
        acc = jnp.zeros((BLK, BLK), F32)
        for block in blocks:
            part = block[f * BLK : (f + 1) * BLK]
            acc = acc + part * part
        rows.append(jnp.sum(acc, axis=0, keepdims=True))
    both = jnp.concatenate(rows + rows + rows + rows, axis=0)
    return (both + pltpu.roll(both, COLS, 1))[0:2]


def first_combine(recv_ref, out_ref, inverse_ref):
    powers = joined_rows(recv_ref[:, FREQ_DEV * BLK :, :])
    inverse = lax.rsqrt(powers)
    for f in range(FREQ_DEV):
        total = jnp.sum(recv_ref[:, f * BLK : (f + 1) * BLK, :].astype(F32), axis=0)
        column = jnp.broadcast_to(to_column(inverse[f : f + 1]), (BLK, BLK))
        inverse_ref[f * BLK : (f + 1) * BLK, :] = column
        out_ref[f * BLK : (f + 1) * BLK, :] = (total * column).astype(BF16)


def second_combine(recv_ref, inverse_ref, scaled_ref, own_ref, msg_ref, *, images):
    means = joined_rows(recv_ref[:, FREQ_DEV * BLK :, :]) / images
    factor = lax.rsqrt(means + 1e-06)
    values = []
    for f in range(FREQ_DEV):
        total = jnp.sum(recv_ref[:, f * BLK : (f + 1) * BLK, :].astype(F32), axis=0)
        value = total * inverse_ref[f * BLK : (f + 1) * BLK, :] * factor[f : f + 1]
        scaled_ref[f * BLK : (f + 1) * BLK, :] = value
        values.append(value)
    value = jnp.concatenate(values, axis=0)
    own = value.astype(BF16)
    own_ref[...] = own
    extra = split_rows(block_sums([value]))
    for k in range(YC):
        msg_ref[k, : FREQ_DEV * BLK, :] = own
        msg_ref[k, FREQ_DEV * BLK :, :] = extra


def sums_kernel(recv_ref, out_ref):
    total = jnp.sum(recv_ref[...].astype(F32), axis=0)
    total = (total + pltpu.roll(total, EXTRA - 2, 0))[0:8]
    for z in range(Z):
        out_ref[z] = total


def gram_kernel(place, rows_ref, mask_ref, sums_ref, scaled_ref, *refs, images, freqs):
    col_refs = refs[:Z]
    out_ref, vec_ref, mask_rows = refs[Z:]
    step = pl.program_id(0)
    means = jnp.sum(sums_ref[...], axis=0)[0:2] / images
    factor = lax.rsqrt(means + 1e-06)
    square = factor * factor

    @pl.when(step == 0)
    def _():
        for f in range(FREQ_DEV):
            vec_ref[f] = (scaled_ref[f * BLK : (f + 1) * BLK, :] * factor[f : f + 1]).astype(BF16)

    load_masks(mask_ref, mask_rows, step)
    lefts = []
    for f in range(FREQ_DEV):
        block = (rows_ref[0, f * BLK : (f + 1) * BLK, :].astype(F32) * square[f : f + 1]).astype(
            BF16
        )
        lefts.append(jnp.concatenate([block, swapped_back(block)], axis=0))
    for z in range(Z):
        total = jnp.zeros((BLK, BLK), F32)
        for f in range(FREQ_DEV):
            gram = nt_dot(lefts[f], col_refs[z][f * BLK : (f + 1) * BLK, :])
            total = total + gram[:BLK] * gram[:BLK] + gram[BLK:] * gram[BLK:]
        where = (place[1] - z) & (Z - 1)
        mask = mask_rows[pl.ds(where, 1), :] * (1.0 / (COLS * freqs))
        value = (total * mask).astype(BF16)
        for x in range(4):
            out_ref[x, 0, where] = value[x * 32 : (x + 1) * 32]


def final_sum(tiles_ref, out_ref):
    for y in range(4):
        for z in range(Z // 2):
            total = tiles_ref[0, y, 0, z].astype(F32)
            for x in range(1, 4):
                total = total + tiles_ref[x, y, 0, z].astype(F32)
            out_ref[0, z, y] = total


def exchange(pieces, axes):
    return lax.all_to_all(pieces, axes, 0, 0, tiled=True)


def shifted(block, by):
    size = lax.axis_size("row_0")
    return lax.ppermute(block, "row_0", [(i, (i + by) % size) for i in range(size)])


def near(block):
    return [block] + [shifted(block, by) for by in (1, 2, -2, -1)]


def far(blocks):
    own, one, two, back_two, back_one = blocks
    three = shifted(two, 1)
    back_three = shifted(back_two, -1)
    four = shifted(two, 2)
    return [own, one, two, three, four, back_three, back_two, back_one]


def body(spectra, basis, start_vectors, pattern):
    group_devices = lax.axis_size("freq")
    images = BLK * lax.axis_size(ROW_COL)
    freq_total = FREQ_DEV * group_devices
    place = jnp.stack([lax.axis_index("col"), lax.axis_index("row_0")]).astype(jnp.int32)
    start = jnp.transpose(start_vectors, (1, 0, 2)).reshape(FREQ_DEV * BLK, 2 * COLS)
    first = near(start)
    dft_table = make_table(ANG, freq_total)
    angular = lax.dot_general(
        dft_table, spectra[:, 0], (((0,), (1,)), ((), ())), preferred_element_type=jnp.float32
    ).astype(jnp.bfloat16)
    radial = lax.dot_general(
        angular, basis, (((3,), (0,)), ((), ())), preferred_element_type=jnp.float32
    ).astype(jnp.bfloat16)
    coef_local = jnp.transpose(radial, (1, 2, 0, 3)).reshape(
        group_devices, FREQ_DEV, IMG_DEV, 2 * COMP
    )
    regrouped = exchange(coef_local, "freq")
    kept = jnp.transpose(pattern.reshape(2, Z, YC // 2), (2, 0, 1)).reshape(YC // 2, 1, EXTRA, 1)
    kept = jnp.broadcast_to(kept.astype(BF16), (YC // 2, 2, EXTRA, BLK)).reshape(YC, EXTRA, BLK)
    regrouped, kept, first = lax.optimization_barrier((regrouped, kept, first))
    own_shape = (FREQ_DEV * BLK, BLK)
    own_type = jax.ShapeDtypeStruct(own_shape, BF16)
    msg_shape = jax.ShapeDtypeStruct((YC, MSG, BLK), BF16)
    big = pltpu.CompilerParams(vmem_limit_bytes=16 << 20)
    small = pltpu.CompilerParams(vmem_limit_bytes=6 << 20)
    own, to_yc = pl.pallas_call(
        prepare,
        out_shape=[own_type, msg_shape],
        scratch_shapes=[pltpu.VMEM(own_shape, F32)],
        compiler_params=small,
        name="prepare",
    )(regrouped, kept)
    rows = exchange(to_yc, YCOL)
    cols = far(near(own))
    first = far(first)

    row_spec = pl.BlockSpec((1, FREQ_DEV * BLK, BLK), lambda i, c: (i, 0, 0))
    mask_spec = pl.BlockSpec((1, EXTRA, BLK), lambda i, c: (i // 2 * 2 + c[0], 16, 0))
    held = pl.BlockSpec(memory_space=pltpu.VMEM)
    stack = pltpu.VMEM((FREQ_DEV, 2 * SPAN, BLK), BF16)
    mask_rows = pltpu.VMEM((Z, BLK), F32)
    kernels, partial = pl.pallas_call(
        cross_kernel,
        grid_spec=pltpu.PrefetchScalarGridSpec(
            num_scalar_prefetch=1,
            grid=(YC,),
            in_specs=[row_spec, mask_spec] + [held] * (2 * Z),
            out_specs=[
                pl.BlockSpec((1, FREQ_DEV, BLK, 2 * SPAN), lambda i, c: (i, 0, 0, 0)),
                pl.BlockSpec((1, MSG, BLK), lambda i, c: (i, 0, 0)),
            ],
            scratch_shapes=[stack, mask_rows],
        ),
        out_shape=[jax.ShapeDtypeStruct((YC, FREQ_DEV, BLK, 2 * SPAN), BF16), msg_shape],
        compiler_params=big,
        name="cross",
    )(place, rows, rows, *cols, *first)
    got = exchange(partial, YCOL)
    own, inverse = pl.pallas_call(
        first_combine,
        out_shape=[own_type, jax.ShapeDtypeStruct(own_shape, F32)],
        compiler_params=small,
        name="combine_one",
    )(got)
    cols = far(near(own))
    partial = pl.pallas_call(
        product_kernel,
        grid=(YC,),
        in_specs=[pl.BlockSpec((1, FREQ_DEV, BLK, 2 * SPAN), lambda i: (i, 0, 0, 0))]
        + [held] * Z,
        out_specs=pl.BlockSpec((1, MSG, BLK), lambda i: (i, 0, 0)),
        out_shape=msg_shape,
        scratch_shapes=[stack, pltpu.VMEM((EXTRA, BLK), BF16)],
        compiler_params=big,
        name="product",
    )(kernels, *cols)
    got = exchange(partial, YCOL)
    scaled, own, to_yc = pl.pallas_call(
        lambda *refs: second_combine(*refs, images=images),
        out_shape=[jax.ShapeDtypeStruct(own_shape, F32), own_type, msg_shape],
        compiler_params=small,
        name="combine_two",
    )(got, inverse)
    last_rows = exchange(to_yc, YCOL)
    cols = far(near(own))
    sums = pl.pallas_call(
        sums_kernel,
        grid=(1,),
        in_specs=[pl.BlockSpec((YC, EXTRA, BLK), lambda i: (0, 16, 0))],
        out_specs=pl.BlockSpec((Z, 8, BLK), lambda i: (0, 0, 0)),
        out_shape=jax.ShapeDtypeStruct((Z, 8, BLK), F32),
        compiler_params=small,
        name="sums",
    )(last_rows)
    sums = exchange(sums, "row_0")
    tiles, vectors = pl.pallas_call(
        lambda *refs: gram_kernel(*refs, images=images, freqs=freq_total),
        grid_spec=pltpu.PrefetchScalarGridSpec(
            num_scalar_prefetch=1,
            grid=(YC,),
            in_specs=[row_spec, mask_spec] + [held] * (2 + Z),
            out_specs=[
                pl.BlockSpec((4, 1, Z, 32, BLK), lambda i, c: (0, i, 0, 0, 0)),
                pl.BlockSpec((FREQ_DEV, BLK, BLK), lambda i, c: (0, 0, 0)),
            ],
            scratch_shapes=[mask_rows],
        ),
        out_shape=[
            jax.ShapeDtypeStruct((4, YC, Z, 32, BLK), BF16),
            jax.ShapeDtypeStruct((FREQ_DEV, BLK, BLK), BF16),
        ],
        compiler_params=big,
        name="gram",
    )(place, last_rows, rows, sums, scaled, *cols)
    arrived = exchange(tiles.reshape(16, 2, Z, 32, BLK), ("freq", "row_1"))
    arrived, vectors = lax.optimization_barrier((arrived, vectors))
    vectors = jnp.transpose(vectors, (1, 0, 2))
    affinity = pl.pallas_call(
        final_sum,
        grid=(2, 2),
        in_specs=[pl.BlockSpec((4, 4, 1, Z // 2, 32, BLK), lambda t, h: (0, 0, t, h, 0, 0))],
        out_specs=pl.BlockSpec((1, Z // 2, 4, 32, BLK), lambda t, h: (t, h, 0, 0, 0)),
        out_shape=jax.ShapeDtypeStruct((2, Z, 4, 32, BLK), F32),
        compiler_params=small,
        name="final",
    )(arrived.reshape(4, 4, 2, Z, 32, BLK))
    return (vectors, affinity.reshape(2, 32, 1, 1, 32, BLK))


def solution(mesh):
    split = Mesh(
        mesh.devices.reshape(mesh.shape["freq"], 8, 4, mesh.shape["col"]),
        ("freq", "row_0", "row_1", "col"),
    )
    placed = (
        P(ROW_COL, "freq", None, None),
        P(),
        P(ROW_COL, "freq", None),
        P(ROW, None, "col", None),
    )
    return jax.shard_map(
        body,
        mesh=split,
        in_specs=placed,
        out_specs=(P(ROW_COL, "freq", None), P(ROW, None, "col", None, "freq", None)),
        check_vma=False,
    )
```

```python
import math

import jax
import jax.numpy as jnp
from jax import lax
from jax.experimental import pallas as pl
from jax.experimental.pallas import tpu as pltpu
from jax.sharding import Mesh
from jax.sharding import PartitionSpec as P

ANG = 128
COMP = 64
COLS = 64
BLK = 128
FREQ_DEV = 2
IMG_DEV = 32
Z = 8
Y = 4
PAIR = 2 * BLK
EXTRA = 16
KEPT = 4 * Z
MSG = PAIR + EXTRA
ROW = ("row_0", "row_1")
ROW_COL = ("row_0", "row_1", "col")
F32 = jnp.float32
BF16 = jnp.bfloat16


def make_table(angles, freq_count):
    angle_ids = jnp.arange(angles, dtype=jnp.int32)
    orders = jnp.arange(freq_count, dtype=jnp.int32) + 1
    phase_steps = angle_ids[:, None] * orders[None, :] % angles
    phase_angle = phase_steps.astype(jnp.float32) * (2.0 * math.pi / angles)
    table_scale = 1.0 / math.sqrt(angles)
    return jnp.stack(
        [jnp.cos(phase_angle) * table_scale, -jnp.sin(phase_angle) * table_scale], axis=1
    ).astype(jnp.bfloat16)


def nt_dot(left, right):
    return lax.dot_general(
        left, right, (((1,), (1,)), ((), ())), preferred_element_type=jnp.float32
    )


def lane_signs(shape):
    lanes = lax.broadcasted_iota(jnp.int32, shape, len(shape) - 1)
    return jnp.where(lanes < COMP, -1.0, 1.0).astype(F32)


def swapped(block):
    wide = block.astype(F32)
    return (pltpu.roll(wide, COMP, 1) * lane_signs(wide.shape)).astype(BF16)


def swapped_back(block):
    wide = block.astype(F32)
    return (pltpu.roll(wide, COMP, 1) * -lane_signs(wide.shape)).astype(BF16)


def split_rows(rows):
    high = rows.astype(BF16)
    low = (rows - high.astype(F32)).astype(BF16)
    zeros = jnp.zeros((EXTRA - 4, BLK), BF16)
    return jnp.concatenate([high.astype(F32), low.astype(F32), zeros.astype(F32)], axis=0).astype(
        BF16
    )


def joined_rows(extra):
    total = jnp.sum(extra.astype(F32), axis=0)
    return total[0:2] + total[2:4]


def to_column(row):
    rows = lax.broadcasted_iota(jnp.int32, (BLK, BLK), 0)
    cols = lax.broadcasted_iota(jnp.int32, (BLK, BLK), 1)
    return jnp.sum(jnp.where(rows == cols, row, 0.0), axis=1, keepdims=True)


def load_stack(stack_ref, col_refs):
    for z in range(Z):
        block = col_refs[z][...]
        twice = swapped(block) * jnp.asarray(2.0, BF16)
        stack_ref[z * 2 * PAIR : z * 2 * PAIR + PAIR, :] = block
        stack_ref[z * 2 * PAIR + PAIR : (z + 1) * 2 * PAIR, :] = twice


def prepare(coef_ref, kept_ref, own_ref, msg_ref, wide_ref):
    for q in range(4):
        for b in range(2):
            wide_ref[pl.ds(b * BLK + q, IMG_DEV, stride=4), :] = coef_ref[q * 2 + b].astype(F32)
    own = wide_ref[...].astype(BF16)
    own_ref[...] = own
    for k in range(Y):
        msg_ref[k, :PAIR, :] = own
        msg_ref[k, PAIR:, :] = kept_ref[k]


def cross_kernel(place, rows_ref, mask_ref, *refs):
    col_refs, first_refs = refs[:Z], refs[Z : 2 * Z]
    kern_ref, msg_ref, stack_ref, mask_rows = refs[2 * Z :]
    step = pl.program_id(0)

    @pl.when(step == 0)
    def _():
        load_stack(stack_ref, first_refs)

    mask_rows[...] = mask_ref[0].astype(F32)
    powers = []
    for b in range(2):
        block = rows_ref[0, b * BLK : (b + 1) * BLK, :] * jnp.asarray(1.0 / COMP, BF16)
        left = jnp.concatenate([block, swapped_back(block)], axis=0)
        acc = jnp.zeros((BLK, BLK), F32)
        for z in range(Z):
            base = b * 2 * Z + 2 * ((place[1] - z) & (Z - 1))
            masked = [
                col_refs[z][h * BLK : (h + 1) * BLK, :]
                * mask_rows[pl.ds(base + h, 1), :].astype(BF16)
                for h in range(2)
            ]
            cross = nt_dot(left, jnp.concatenate(masked, axis=0))
            re = cross[:BLK]
            im = cross[BLK:]
            re2 = re * re
            im2 = im * im
            at = z * 2 * PAIR
            kern_ref[step, b, :, at : at + PAIR] = (re2 - im2).astype(BF16)
            kern_ref[step, b, :, at + PAIR : at + 2 * PAIR] = (re * im).astype(BF16)
            mag = re2 + im2
            mag = mag * mag
            acc = acc + mag[:, :BLK] + mag[:, BLK:]
        high = acc.astype(BF16)
        low = (acc - high.astype(F32)).astype(BF16)
        ones = jnp.ones((EXTRA, BLK), BF16)
        powers.append((nt_dot(ones, high) + nt_dot(ones, low))[0:1])
    kernel = kern_ref[step].reshape(PAIR, 2 * Z * PAIR)
    product = jnp.dot(kernel, stack_ref[...], preferred_element_type=F32)
    msg_ref[0, :PAIR, :] = product.astype(BF16)
    msg_ref[0, PAIR:, :] = split_rows(jnp.concatenate(powers, axis=0))


def product_kernel(kern_ref, *refs):
    col_refs = refs[:Z]
    msg_ref, stack_ref, sums_ref = refs[Z:]
    step = pl.program_id(0)

    @pl.when(step == 0)
    def _():
        load_stack(stack_ref, col_refs)
        sums_ref[...] = split_rows(block_sums([ref[...].astype(F32) for ref in col_refs]))

    kernel = kern_ref[step].reshape(PAIR, 2 * Z * PAIR)
    product = jnp.dot(kernel, stack_ref[...], preferred_element_type=F32)
    msg_ref[0, :PAIR, :] = product.astype(BF16)
    msg_ref[0, PAIR:, :] = sums_ref[...]


def block_sums(blocks):
    rows = []
    for b in range(2):
        acc = jnp.zeros((BLK, BLK), F32)
        for block in blocks:
            part = block[b * BLK : (b + 1) * BLK]
            acc = acc + part * part
        rows.append(jnp.sum(acc, axis=0, keepdims=True))
    both = jnp.concatenate(rows + rows + rows + rows, axis=0)
    return (both + pltpu.roll(both, COLS, 1))[0:2]


def first_combine(recv_ref, out_ref, inverse_ref):
    powers = joined_rows(recv_ref[:, PAIR:, :])
    inverse = lax.rsqrt(powers)
    for b in range(2):
        total = jnp.sum(recv_ref[:, b * BLK : (b + 1) * BLK, :].astype(F32), axis=0)
        column = jnp.broadcast_to(to_column(inverse[b : b + 1]), (BLK, BLK))
        inverse_ref[b * BLK : (b + 1) * BLK, :] = column
        out_ref[b * BLK : (b + 1) * BLK, :] = (total * column).astype(BF16)


def second_combine(recv_ref, inverse_ref, scaled_ref, own_ref, msg_ref, *, images):
    means = joined_rows(recv_ref[:, PAIR:, :]) / images
    factor = lax.rsqrt(means[0:1] + means[1:2] + 1e-06)
    total = jnp.sum(recv_ref[:, :PAIR, :].astype(F32), axis=0)
    value = total * inverse_ref[...] * factor
    scaled_ref[...] = value
    own = value.astype(BF16)
    own_ref[...] = own
    extra = split_rows(block_sums([value]))
    for k in range(Y):
        msg_ref[k, :PAIR, :] = own
        msg_ref[k, PAIR:, :] = extra


def sums_kernel(recv_ref, out_ref):
    total = jnp.sum(recv_ref[...].astype(F32), axis=0)
    total = total + pltpu.roll(total, EXTRA - 2, 0)
    total = (total + pltpu.roll(total, EXTRA - 1, 0))[0:8]
    for k in range(2 * Z):
        out_ref[k] = total


def pack_kernel(place, rows_ref, *refs):
    col_refs, out_ref = refs[:Z], refs[Z]
    other = pl.multiple_of((1 - place[0]) * BLK, BLK)
    for k in range(Y):
        out_ref[k * PAIR : (k + 1) * PAIR, :] = rows_ref[k, :PAIR, :]
    for z in range(Z):
        at = Y * PAIR + z * BLK
        out_ref[at : at + BLK, :] = col_refs[z][pl.ds(other, BLK), :]


def gram_kernel(
    place, rows_ref, mask_ref, sums_ref, scaled_ref, got_ref, *refs, images, freqs
):
    col_refs = refs[:Z]
    out_ref, vec_ref, mask_rows = refs[Z:]
    step = pl.program_id(0)
    totals = []
    for c in range(2):
        total = sums_ref[c]
        for z in range(1, Z):
            total = total + sums_ref[2 * z + c]
        totals.append(lax.rsqrt(total[0:1] / images + 1e-06))
    first = place[0] == 0
    factor = jnp.where(first, totals[0], totals[1])
    factor_other = jnp.where(first, totals[1], totals[0])
    mine = pl.multiple_of(place[0] * BLK, BLK)

    @pl.when(step == 0)
    def _():
        vec_ref[place[0]] = (scaled_ref[pl.ds(mine, BLK), :] * factor).astype(BF16)
        own_row = pl.multiple_of((place[2] * 2 + place[0]) * BLK, BLK)
        block = got_ref[pl.ds(own_row, BLK), :].astype(F32)
        vec_ref[1 - place[0]] = (block * factor_other).astype(BF16)

    mask_rows[...] = mask_ref[0].astype(F32)
    for b in range(2):
        at = pl.multiple_of(step * PAIR + b * BLK, BLK)
        sources = (
            (rows_ref[0, b * BLK : (b + 1) * BLK, :], factor),
            (got_ref[pl.ds(at, BLK), :], factor_other),
        )
        lefts = []
        for rows, scale in sources:
            block = (rows.astype(F32) * (scale * scale)).astype(BF16)
            lefts.append(jnp.concatenate([block, swapped_back(block)], axis=0))
        for z in range(Z):
            far = Y * PAIR + z * BLK
            total = jnp.zeros((BLK, BLK), F32)
            for left, right in zip(
                lefts, (col_refs[z][pl.ds(mine, BLK), :], got_ref[far : far + BLK, :])
            ):
                gram = nt_dot(left, right)
                total = total + gram[:BLK] * gram[:BLK] + gram[BLK:] * gram[BLK:]
            where = (place[1] - z) & (Z - 1)
            mask = mask_rows[pl.ds(b * 2 * Z + 2 * where + place[0], 1), :]
            value = (total * (mask * (1.0 / (COLS * freqs)))).astype(BF16)
            for x in range(4):
                out_ref[x, 0, b, where] = value[x * 32 : (x + 1) * 32]


def final_sum(tiles_ref, out_ref):
    for y in range(4):
        for z in range(Z // 2):
            total = tiles_ref[0, y, 0, z].astype(F32)
            for x in range(1, 4):
                total = total + tiles_ref[x, y, 0, z].astype(F32)
            out_ref[0, z, y] = total


def exchange(pieces, axes):
    return lax.all_to_all(pieces, axes, 0, 0, tiled=True)


def shifted(block, by):
    size = lax.axis_size("row_0")
    return lax.ppermute(block, "row_0", [(i, (i + by) % size) for i in range(size)])


def near(block):
    return [block] + [shifted(block, by) for by in (1, 2, -2, -1)]


def far(blocks):
    own, one, two, back_two, back_one = blocks
    three = shifted(two, 1)
    back_three = shifted(back_two, -1)
    four = shifted(two, 2)
    return [own, one, two, three, four, back_three, back_two, back_one]


def body(spectra, basis, start_vectors, pattern):
    group_devices = lax.axis_size("freq")
    images = BLK * lax.axis_size(ROW_COL)
    freq_total = FREQ_DEV * group_devices
    col = lax.axis_index("col")
    place = jnp.stack([col, lax.axis_index("row_0"), lax.axis_index("row_1")]).astype(jnp.int32)
    dft_table = make_table(ANG, freq_total)
    angular = lax.dot_general(
        dft_table, spectra[:, 0], (((0,), (1,)), ((), ())), preferred_element_type=jnp.float32
    ).astype(jnp.bfloat16)
    radial = lax.dot_general(
        angular, basis, (((3,), (0,)), ((), ())), preferred_element_type=jnp.float32
    ).astype(jnp.bfloat16)
    coef_local = jnp.transpose(radial, (1, 2, 0, 3)).reshape(freq_total, IMG_DEV, 2 * COMP)
    start = jnp.transpose(start_vectors, (1, 0, 2))
    here = jnp.where(col == 0, start[0], start[1])
    there = jnp.where(col == 0, start[1], start[0])
    there = lax.ppermute(there, "col", [(0, 1), (1, 0)])
    start = jnp.concatenate(
        [jnp.where(col == 0, here, there), jnp.where(col == 0, there, here)], axis=0
    )
    flags = pattern.reshape(2, Z, Y).astype(BF16)
    flags = jnp.broadcast_to(flags.reshape(2 * Z * Y, 1), (2 * Z * Y, BLK))
    flags_other = lax.ppermute(flags, "col", [(0, 1), (1, 0)])
    regrouped = exchange(coef_local, ("freq", "col"))
    both = [jnp.where(col == 0, flags, flags_other), jnp.where(col == 0, flags_other, flags)]
    kept = jnp.stack([flag.reshape(2, Z, Y, BLK) for flag in both], axis=2)
    kept = jnp.transpose(kept, (3, 0, 1, 2, 4)).reshape(Y, KEPT, BLK)
    first = near(start)
    regrouped, kept, first = lax.optimization_barrier((regrouped, kept, first))
    own_shape = (PAIR, BLK)
    own_type = jax.ShapeDtypeStruct(own_shape, BF16)
    msg_shape = jax.ShapeDtypeStruct((Y, MSG, BLK), BF16)
    big = pltpu.CompilerParams(vmem_limit_bytes=24 << 20)
    small = pltpu.CompilerParams(vmem_limit_bytes=6 << 20)
    own, to_y = pl.pallas_call(
        prepare,
        out_shape=[own_type, jax.ShapeDtypeStruct((Y, PAIR + KEPT, BLK), BF16)],
        scratch_shapes=[pltpu.VMEM(own_shape, F32)],
        compiler_params=small,
        name="prepare",
    )(regrouped, kept)
    rows = exchange(to_y, "row_1")
    cols = far(near(own))
    first = far(first)

    row_spec = pl.BlockSpec((1, PAIR, BLK), lambda i, p: (i, 0, 0))
    mask_spec = pl.BlockSpec((1, KEPT, BLK), lambda i, p: (i, PAIR // KEPT, 0))
    held = pl.BlockSpec(memory_space=pltpu.VMEM)
    stack = pltpu.VMEM((2 * Z * PAIR, BLK), BF16)
    mask_rows = pltpu.VMEM((KEPT, BLK), F32)
    kernels, partial = pl.pallas_call(
        cross_kernel,
        grid_spec=pltpu.PrefetchScalarGridSpec(
            num_scalar_prefetch=1,
            grid=(Y,),
            in_specs=[row_spec, mask_spec] + [held] * (2 * Z),
            out_specs=[held, pl.BlockSpec((1, MSG, BLK), lambda i, p: (i, 0, 0))],
            scratch_shapes=[stack, mask_rows],
        ),
        out_shape=[jax.ShapeDtypeStruct((Y, 2, BLK, 2 * Z * PAIR), BF16), msg_shape],
        compiler_params=big,
        name="cross",
    )(place, rows, rows, *cols, *first)
    got = exchange(partial, "row_1")
    own, inverse = pl.pallas_call(
        first_combine,
        out_shape=[own_type, jax.ShapeDtypeStruct(own_shape, F32)],
        compiler_params=small,
        name="combine_one",
    )(got)
    cols = far(near(own))
    partial = pl.pallas_call(
        product_kernel,
        grid=(Y,),
        in_specs=[held] * (1 + Z),
        out_specs=pl.BlockSpec((1, MSG, BLK), lambda i: (i, 0, 0)),
        out_shape=msg_shape,
        scratch_shapes=[stack, pltpu.VMEM((EXTRA, BLK), BF16)],
        compiler_params=big,
        name="product",
    )(kernels, *cols)
    got = exchange(partial, "row_1")
    scaled, own, to_y = pl.pallas_call(
        lambda *refs: second_combine(*refs, images=images),
        out_shape=[jax.ShapeDtypeStruct(own_shape, F32), own_type, msg_shape],
        compiler_params=small,
        name="combine_two",
    )(got, inverse)
    last_rows = exchange(to_y, "row_1")
    cols = far(near(own))
    sums = pl.pallas_call(
        sums_kernel,
        grid=(1,),
        in_specs=[pl.BlockSpec((Y, EXTRA, BLK), lambda i: (0, PAIR // EXTRA, 0))],
        out_specs=pl.BlockSpec((2 * Z, 8, BLK), lambda i: (0, 0, 0)),
        out_shape=jax.ShapeDtypeStruct((2 * Z, 8, BLK), F32),
        compiler_params=small,
        name="sums",
    )(last_rows)
    sums = exchange(sums, ("row_0", "col"))
    packed = pl.pallas_call(
        pack_kernel,
        in_specs=[pl.BlockSpec(memory_space=pltpu.SMEM)] + [held] * (1 + Z),
        out_shape=jax.ShapeDtypeStruct((Y * PAIR + Z * BLK, BLK), BF16),
        compiler_params=small,
        name="pack",
    )(place, last_rows, *cols)
    packed = lax.ppermute(packed, "col", [(0, 1), (1, 0)])
    tiles, vectors = pl.pallas_call(
        lambda *refs: gram_kernel(*refs, images=images, freqs=freq_total),
        grid_spec=pltpu.PrefetchScalarGridSpec(
            num_scalar_prefetch=1,
            grid=(Y,),
            in_specs=[row_spec, mask_spec] + [held] * (3 + Z),
            out_specs=[
                pl.BlockSpec((4, 1, 2, Z, 32, BLK), lambda i, p: (0, i, 0, 0, 0, 0)),
                pl.BlockSpec((FREQ_DEV, BLK, BLK), lambda i, p: (0, 0, 0)),
            ],
            scratch_shapes=[mask_rows],
        ),
        out_shape=[
            jax.ShapeDtypeStruct((4, Y, 2, Z, 32, BLK), BF16),
            jax.ShapeDtypeStruct((FREQ_DEV, BLK, BLK), BF16),
        ],
        compiler_params=big,
        name="gram",
    )(place, last_rows, rows, sums, scaled, packed, *cols)
    arrived = exchange(tiles.reshape(16, 2, Z, 32, BLK), ("freq", "row_1"))
    arrived, vectors = lax.optimization_barrier((arrived, vectors))
    vectors = jnp.transpose(vectors, (1, 0, 2))
    affinity = pl.pallas_call(
        final_sum,
        grid=(2, 2),
        in_specs=[pl.BlockSpec((4, 4, 1, Z // 2, 32, BLK), lambda t, h: (0, 0, t, h, 0, 0))],
        out_specs=pl.BlockSpec((1, Z // 2, 4, 32, BLK), lambda t, h: (t, h, 0, 0, 0)),
        out_shape=jax.ShapeDtypeStruct((2, Z, 4, 32, BLK), F32),
        compiler_params=small,
        name="final",
    )(arrived.reshape(4, 4, 2, Z, 32, BLK))
    return (vectors, affinity.reshape(2, 32, 1, 1, 32, BLK))


def solution(mesh):
    split = Mesh(
        mesh.devices.reshape(mesh.shape["freq"], 8, 4, mesh.shape["col"]),
        ("freq", "row_0", "row_1", "col"),
    )
    placed = (
        P(ROW_COL, "freq", None, None),
        P(),
        P(ROW_COL, "freq", None),
        P(ROW, None, "col", None),
    )
    return jax.shard_map(
        body,
        mesh=split,
        in_specs=placed,
        out_specs=(P(ROW_COL, "freq", None), P(ROW, None, "col", None, "freq", None)),
        check_vma=False,
    )
```

```python
import math

import jax
import jax.numpy as jnp
from jax import lax
from jax.experimental import pallas as pl
from jax.experimental.pallas import tpu as pltpu
from jax.sharding import Mesh
from jax.sharding import PartitionSpec as P

ANG = 128
COMP = 64
COLS = 64
BLK = 128
FREQ_DEV = 2
IMG_DEV = 32
Z = 8
X = 4
Y = 4
PAIR = 2 * BLK
EXTRA = 16
KEPT = 4 * Z
ROWS = X * Y * PAIR
MSG = PAIR + EXTRA
ROW = ("row_0", "row_1")
ROW_COL = ("row_0", "row_1", "col")
F32 = jnp.float32
BF16 = jnp.bfloat16


def make_table(angles, freq_count):
    angle_ids = jnp.arange(angles, dtype=jnp.int32)
    orders = jnp.arange(freq_count, dtype=jnp.int32) + 1
    phase_steps = angle_ids[:, None] * orders[None, :] % angles
    phase_angle = phase_steps.astype(jnp.float32) * (2.0 * math.pi / angles)
    table_scale = 1.0 / math.sqrt(angles)
    return jnp.stack(
        [jnp.cos(phase_angle) * table_scale, -jnp.sin(phase_angle) * table_scale], axis=1
    ).astype(jnp.bfloat16)


def nt_dot(left, right):
    return lax.dot_general(
        left, right, (((1,), (1,)), ((), ())), preferred_element_type=jnp.float32
    )


def lane_signs(shape):
    lanes = lax.broadcasted_iota(jnp.int32, shape, len(shape) - 1)
    return jnp.where(lanes < COMP, -1.0, 1.0).astype(F32)


def swapped(block):
    wide = block.astype(F32)
    return (pltpu.roll(wide, COMP, 1) * lane_signs(wide.shape)).astype(BF16)


def swapped_back(block):
    wide = block.astype(F32)
    return (pltpu.roll(wide, COMP, 1) * -lane_signs(wide.shape)).astype(BF16)


def split_rows(rows):
    high = rows.astype(BF16)
    low = (rows - high.astype(F32)).astype(BF16)
    zeros = jnp.zeros((EXTRA - 4, BLK), BF16)
    return jnp.concatenate([high.astype(F32), low.astype(F32), zeros.astype(F32)], axis=0).astype(
        BF16
    )


def joined_rows(extra):
    total = jnp.sum(extra.astype(F32), axis=0)
    return total[0:2] + total[2:4]


def to_column(row):
    rows = lax.broadcasted_iota(jnp.int32, (BLK, BLK), 0)
    cols = lax.broadcasted_iota(jnp.int32, (BLK, BLK), 1)
    return jnp.sum(jnp.where(rows == cols, row, 0.0), axis=1, keepdims=True)


def load_stack(stack_ref, col_refs):
    for z in range(Z):
        block = col_refs[z][...]
        twice = swapped(block) * jnp.asarray(2.0, BF16)
        stack_ref[z * 2 * PAIR : z * 2 * PAIR + PAIR, :] = block
        stack_ref[z * 2 * PAIR + PAIR : (z + 1) * 2 * PAIR, :] = twice


def prepare(coef_ref, kept_ref, own_ref, msg_ref, wide_ref):
    for q in range(4):
        for b in range(2):
            wide_ref[pl.ds(b * BLK + q, IMG_DEV, stride=4), :] = coef_ref[q * 2 + b].astype(F32)
    own = wide_ref[...].astype(BF16)
    own_ref[...] = own
    for k in range(Y):
        msg_ref[k, :PAIR, :] = own
        msg_ref[k, PAIR:, :] = kept_ref[k]


def cross_kernel(place, rows_ref, mask_ref, *refs):
    col_refs, first_refs = refs[:Z], refs[Z : 2 * Z]
    kern_ref, msg_ref, stack_ref, mask_rows = refs[2 * Z :]
    step = pl.program_id(0)

    @pl.when(step == 0)
    def _():
        load_stack(stack_ref, first_refs)

    mask_rows[...] = mask_ref[0].astype(F32)
    powers = []
    for b in range(2):
        block = rows_ref[0, b * BLK : (b + 1) * BLK, :] * jnp.asarray(1.0 / COMP, BF16)
        left = jnp.concatenate([block, swapped_back(block)], axis=0)
        acc = jnp.zeros((BLK, BLK), F32)
        for z in range(Z):
            base = b * 2 * Z + 2 * ((place[1] - z) & (Z - 1))
            masked = [
                col_refs[z][h * BLK : (h + 1) * BLK, :]
                * mask_rows[pl.ds(base + h, 1), :].astype(BF16)
                for h in range(2)
            ]
            cross = nt_dot(left, jnp.concatenate(masked, axis=0))
            re = cross[:BLK]
            im = cross[BLK:]
            re2 = re * re
            im2 = im * im
            at = z * 2 * PAIR
            kern_ref[step, b, :, at : at + PAIR] = (re2 - im2).astype(BF16)
            kern_ref[step, b, :, at + PAIR : at + 2 * PAIR] = (re * im).astype(BF16)
            mag = re2 + im2
            mag = mag * mag
            acc = acc + mag[:, :BLK] + mag[:, BLK:]
        high = acc.astype(BF16)
        low = (acc - high.astype(F32)).astype(BF16)
        ones = jnp.ones((EXTRA, BLK), BF16)
        powers.append((nt_dot(ones, high) + nt_dot(ones, low))[0:1])
    kernel = kern_ref[step].reshape(PAIR, 2 * Z * PAIR)
    product = jnp.dot(kernel, stack_ref[...], preferred_element_type=F32)
    msg_ref[0, :PAIR, :] = product.astype(BF16)
    msg_ref[0, PAIR:, :] = split_rows(jnp.concatenate(powers, axis=0))


def product_kernel(kern_ref, *refs):
    col_refs = refs[:Z]
    msg_ref, stack_ref, sums_ref = refs[Z:]
    step = pl.program_id(0)

    @pl.when(step == 0)
    def _():
        load_stack(stack_ref, col_refs)
        sums_ref[...] = split_rows(block_sums([ref[...].astype(F32) for ref in col_refs]))

    kernel = kern_ref[step].reshape(PAIR, 2 * Z * PAIR)
    product = jnp.dot(kernel, stack_ref[...], preferred_element_type=F32)
    msg_ref[0, :PAIR, :] = product.astype(BF16)
    msg_ref[0, PAIR:, :] = sums_ref[...]


def block_sums(blocks):
    rows = []
    for b in range(2):
        acc = jnp.zeros((BLK, BLK), F32)
        for block in blocks:
            part = block[b * BLK : (b + 1) * BLK]
            acc = acc + part * part
        rows.append(jnp.sum(acc, axis=0, keepdims=True))
    both = jnp.concatenate(rows + rows + rows + rows, axis=0)
    return (both + pltpu.roll(both, COLS, 1))[0:2]


def first_combine(recv_ref, out_ref, inverse_ref):
    powers = joined_rows(recv_ref[:, PAIR:, :])
    inverse = lax.rsqrt(powers)
    for b in range(2):
        total = jnp.sum(recv_ref[:, b * BLK : (b + 1) * BLK, :].astype(F32), axis=0)
        column = jnp.broadcast_to(to_column(inverse[b : b + 1]), (BLK, BLK))
        inverse_ref[b * BLK : (b + 1) * BLK, :] = column
        out_ref[b * BLK : (b + 1) * BLK, :] = (total * column).astype(BF16)


def second_combine(recv_ref, inverse_ref, scaled_ref, own_ref, msg_ref, *, images):
    means = joined_rows(recv_ref[:, PAIR:, :]) / images
    factor = lax.rsqrt(means[0:1] + means[1:2] + 1e-06)
    total = jnp.sum(recv_ref[:, :PAIR, :].astype(F32), axis=0)
    value = total * inverse_ref[...] * factor
    scaled_ref[...] = value
    own = value.astype(BF16)
    own_ref[...] = own
    extra = split_rows(block_sums([value]))
    for k in range(X * Y):
        msg_ref[k, :PAIR, :] = own
        msg_ref[k, PAIR:, :] = extra


def sums_kernel(recv_ref, out_ref):
    rows = []
    for x in range(X):
        total = jnp.sum(recv_ref[x * Y : (x + 1) * Y].astype(F32), axis=0)
        rows.append(jnp.sum(total, axis=0, keepdims=True))
    total = jnp.concatenate(rows + rows, axis=0)
    for k in range(2 * Z):
        out_ref[k] = total


def pack_kernel(place, rows_ref, *refs):
    col_refs, out_ref = refs[: 2 * X], refs[2 * X]
    other = pl.multiple_of((1 - place[0]) * BLK, BLK)
    for k in range(X * Y):
        out_ref[k * PAIR : (k + 1) * PAIR, :] = rows_ref[k, :PAIR, :]
    for k in range(2 * X):
        at = ROWS + k * BLK
        out_ref[at : at + BLK, :] = col_refs[k][pl.ds(other, BLK), :]


def gram_kernel(place, mask_ref, rows_ref, sums_ref, scaled_ref, got_ref, *refs, images, freqs):
    col_refs = refs[: 2 * X]
    out_ref, vec_ref, mask_rows, factors, scaled_cols = refs[2 * X :]
    step = pl.program_id(0)
    core, me_z, me_y, me_x = place[0], place[1], place[2], place[3]
    mine = pl.multiple_of(core * BLK, BLK)

    @pl.when(step == 0)
    def _():
        for c in range(2):
            total = sums_ref[c]
            for z in range(1, Z):
                total = total + sums_ref[2 * z + c]
            factors[c] = lax.rsqrt(total / images + 1e-06)
        mine_factor = factors[core, pl.ds(me_x, 1), :]
        vec_ref[core] = (scaled_ref[pl.ds(mine, BLK), :] * mine_factor).astype(BF16)
        at = pl.multiple_of(((me_x * Y + me_y) * 2 + core) * BLK, BLK)
        block = got_ref[pl.ds(at, BLK), :].astype(F32)
        vec_ref[1 - core] = (block * factors[1 - core, pl.ds(me_x, 1), :]).astype(BF16)
        for r in range(X):
            from_x = (me_x - r) & (X - 1)
            for p in range(2):
                scale = factors[core if p == 0 else 1 - core, pl.ds(from_x, 1), :]
                scale = scale * scale
                for h in range(2):
                    if p == 0:
                        block = col_refs[2 * r + h][pl.ds(mine, BLK), :]
                    else:
                        far_at = ROWS + (2 * r + h) * BLK
                        block = got_ref[far_at : far_at + BLK, :]
                    block = (block.astype(F32) * scale).astype(BF16)
                    scaled_cols[2 * r + p, h * BLK : (h + 1) * BLK, :] = block
                    scaled_cols[2 * r + p, (2 + h) * BLK : (3 + h) * BLK, :] = swapped(block)

    mask_rows[...] = mask_ref[0].astype(F32)
    total = jnp.zeros((PAIR, PAIR), F32)
    for r in range(X):
        source = ((me_x - r) & (X - 1)) * Y + step
        at = pl.multiple_of(source * PAIR, PAIR)
        for p in range(2):
            rows = rows_ref[source, :PAIR, :] if p == 0 else got_ref[pl.ds(at, PAIR), :]
            gram = nt_dot(rows, scaled_cols[2 * r + p])
            total = total + gram[:, :PAIR] * gram[:, :PAIR] + gram[:, PAIR:] * gram[:, PAIR:]
    for b in range(2):
        for h in range(2):
            where = (me_z + 2 * me_x + h) & (Z - 1)
            mask = mask_rows[pl.ds(b * 2 * Z + 2 * where + core, 1), :]
            value = total[b * BLK : (b + 1) * BLK, h * BLK : (h + 1) * BLK]
            value = (value * (mask * (1.0 / (COLS * freqs)))).astype(BF16)
            for x in range(X):
                out_ref[x, 0, b, h] = value[x * 32 : (x + 1) * 32]


def final_spread(place, tiles_ref, out_ref):
    for x in range(X):
        for h in range(2):
            where = (place[1] + 2 * x + h) & (Z - 1)
            for y in range(Y):
                out_ref[0, where, y] = tiles_ref[x * Y + y, 0, h].astype(F32)


def exchange(pieces, axes):
    return lax.all_to_all(pieces, axes, 0, 0, tiled=True)


def shifted(block, by):
    size = lax.axis_size("row_0")
    return lax.ppermute(block, "row_0", [(i, (i + by) % size) for i in range(size)])


def near(block):
    return [block] + [shifted(block, by) for by in (1, 2, -2, -1)]


def far(blocks):
    own, one, two, back_two, back_one = blocks
    three = shifted(two, 1)
    back_three = shifted(back_two, -1)
    four = shifted(two, 2)
    return [own, one, two, three, four, back_three, back_two, back_one]


def last_columns(block):
    found = []
    for r in range(X):
        for h in range(2):
            pairs = []
            for x in range(X):
                for z in range(Z):
                    to_x = (x + r) % X
                    pairs.append((x * Z + z, to_x * Z + (z - 2 * to_x - h) % Z))
            found.append(lax.ppermute(block, ("freq", "row_0"), pairs))
    return found


def body(spectra, basis, start_vectors, pattern):
    group_devices = lax.axis_size("freq")
    images = BLK * lax.axis_size(ROW_COL)
    freq_total = FREQ_DEV * group_devices
    col = lax.axis_index("col")
    places = [col] + [lax.axis_index(name) for name in ("row_0", "row_1", "freq")]
    place = jnp.stack(places).astype(jnp.int32)
    dft_table = make_table(ANG, freq_total)
    angular = lax.dot_general(
        dft_table, spectra[:, 0], (((0,), (1,)), ((), ())), preferred_element_type=jnp.float32
    ).astype(jnp.bfloat16)
    radial = lax.dot_general(
        angular, basis, (((3,), (0,)), ((), ())), preferred_element_type=jnp.float32
    ).astype(jnp.bfloat16)
    coef_local = jnp.transpose(radial, (1, 2, 0, 3)).reshape(freq_total, IMG_DEV, 2 * COMP)
    start = jnp.transpose(start_vectors, (1, 0, 2))
    here = jnp.where(col == 0, start[0], start[1])
    there = jnp.where(col == 0, start[1], start[0])
    there = lax.ppermute(there, "col", [(0, 1), (1, 0)])
    start = jnp.concatenate(
        [jnp.where(col == 0, here, there), jnp.where(col == 0, there, here)], axis=0
    )
    flags = pattern.reshape(2, Z, Y).astype(BF16)
    flags = jnp.broadcast_to(flags.reshape(2 * Z * Y, 1), (2 * Z * Y, BLK))
    flags_other = lax.ppermute(flags, "col", [(0, 1), (1, 0)])
    regrouped = exchange(coef_local, ("freq", "col"))
    both = [jnp.where(col == 0, flags, flags_other), jnp.where(col == 0, flags_other, flags)]
    kept = jnp.stack([flag.reshape(2, Z, Y, BLK) for flag in both], axis=2)
    kept = jnp.transpose(kept, (3, 0, 1, 2, 4)).reshape(Y, KEPT, BLK)
    first = near(start)
    regrouped, kept, first = lax.optimization_barrier((regrouped, kept, first))
    own_shape = (PAIR, BLK)
    own_type = jax.ShapeDtypeStruct(own_shape, BF16)
    msg_shape = jax.ShapeDtypeStruct((Y, MSG, BLK), BF16)
    big = pltpu.CompilerParams(vmem_limit_bytes=24 << 20)
    small = pltpu.CompilerParams(vmem_limit_bytes=6 << 20)
    own, to_y = pl.pallas_call(
        prepare,
        out_shape=[own_type, jax.ShapeDtypeStruct((Y, PAIR + KEPT, BLK), BF16)],
        scratch_shapes=[pltpu.VMEM(own_shape, F32)],
        compiler_params=small,
        name="prepare",
    )(regrouped, kept)
    rows = exchange(to_y, "row_1")
    cols = far(near(own))
    first = far(first)

    row_spec = pl.BlockSpec((1, PAIR, BLK), lambda i, p: (i, 0, 0))
    mask_spec = pl.BlockSpec((1, KEPT, BLK), lambda i, p: (i, PAIR // KEPT, 0))
    held = pl.BlockSpec(memory_space=pltpu.VMEM)
    stack = pltpu.VMEM((2 * Z * PAIR, BLK), BF16)
    mask_rows = pltpu.VMEM((KEPT, BLK), F32)
    kernels, partial = pl.pallas_call(
        cross_kernel,
        grid_spec=pltpu.PrefetchScalarGridSpec(
            num_scalar_prefetch=1,
            grid=(Y,),
            in_specs=[row_spec, mask_spec] + [held] * (2 * Z),
            out_specs=[held, pl.BlockSpec((1, MSG, BLK), lambda i, p: (i, 0, 0))],
            scratch_shapes=[stack, mask_rows],
        ),
        out_shape=[jax.ShapeDtypeStruct((Y, 2, BLK, 2 * Z * PAIR), BF16), msg_shape],
        compiler_params=big,
        name="cross",
    )(place, rows, rows, *cols, *first)
    got = exchange(partial, "row_1")
    own, inverse = pl.pallas_call(
        first_combine,
        out_shape=[own_type, jax.ShapeDtypeStruct(own_shape, F32)],
        compiler_params=small,
        name="combine_one",
    )(got)
    cols = far(near(own))
    partial = pl.pallas_call(
        product_kernel,
        grid=(Y,),
        in_specs=[held] * (1 + Z),
        out_specs=pl.BlockSpec((1, MSG, BLK), lambda i: (i, 0, 0)),
        out_shape=msg_shape,
        scratch_shapes=[stack, pltpu.VMEM((EXTRA, BLK), BF16)],
        compiler_params=big,
        name="product",
    )(kernels, *cols)
    got = exchange(partial, "row_1")
    scaled, own, to_xy = pl.pallas_call(
        lambda *refs: second_combine(*refs, images=images),
        out_shape=[
            jax.ShapeDtypeStruct(own_shape, F32),
            own_type,
            jax.ShapeDtypeStruct((X * Y, MSG, BLK), BF16),
        ],
        compiler_params=small,
        name="combine_two",
    )(got, inverse)
    last_rows = exchange(to_xy, ("freq", "row_1"))
    cols = last_columns(own)
    sums = pl.pallas_call(
        sums_kernel,
        grid=(1,),
        in_specs=[pl.BlockSpec((X * Y, EXTRA, BLK), lambda i: (0, PAIR // EXTRA, 0))],
        out_specs=pl.BlockSpec((2 * Z, 8, BLK), lambda i: (0, 0, 0)),
        out_shape=jax.ShapeDtypeStruct((2 * Z, 8, BLK), F32),
        compiler_params=small,
        name="sums",
    )(last_rows)
    sums, cols = lax.optimization_barrier((sums, cols))
    sums = exchange(sums, ("row_0", "col"))
    packed = pl.pallas_call(
        pack_kernel,
        in_specs=[pl.BlockSpec(memory_space=pltpu.SMEM)] + [held] * (1 + 2 * X),
        out_specs=held,
        out_shape=jax.ShapeDtypeStruct((ROWS + 2 * X * BLK, BLK), BF16),
        compiler_params=small,
        name="pack",
    )(place, last_rows, *cols)
    packed = lax.ppermute(packed, "col", [(0, 1), (1, 0)])
    tiles, vectors = pl.pallas_call(
        lambda *refs: gram_kernel(*refs, images=images, freqs=freq_total),
        grid_spec=pltpu.PrefetchScalarGridSpec(
            num_scalar_prefetch=1,
            grid=(Y,),
            in_specs=[mask_spec] + [held] * (4 + 2 * X),
            out_specs=[
                pl.BlockSpec((X, 1, 2, 2, 32, BLK), lambda i, p: (0, i, 0, 0, 0, 0)),
                pl.BlockSpec((FREQ_DEV, BLK, BLK), lambda i, p: (0, 0, 0)),
            ],
            scratch_shapes=[
                mask_rows,
                pltpu.VMEM((2, 8, BLK), F32),
                pltpu.VMEM((2 * X, 2 * PAIR, BLK), BF16),
            ],
        ),
        out_shape=[
            jax.ShapeDtypeStruct((X, Y, 2, 2, 32, BLK), BF16),
            jax.ShapeDtypeStruct((FREQ_DEV, BLK, BLK), BF16),
        ],
        compiler_params=big,
        name="gram",
    )(place, rows, last_rows, sums, scaled, packed, *cols)
    arrived = exchange(tiles.reshape(X * Y, 2, 2, 32, BLK), ("freq", "row_1"))
    arrived, vectors = lax.optimization_barrier((arrived, vectors))
    vectors = jnp.transpose(vectors, (1, 0, 2))
    affinity = pl.pallas_call(
        final_spread,
        grid_spec=pltpu.PrefetchScalarGridSpec(
            num_scalar_prefetch=1,
            grid=(2,),
            in_specs=[pl.BlockSpec((X * Y, 1, 2, 32, BLK), lambda b, p: (0, b, 0, 0, 0))],
            out_specs=pl.BlockSpec((1, Z, Y, 32, BLK), lambda b, p: (b, 0, 0, 0, 0)),
        ),
        out_shape=jax.ShapeDtypeStruct((2, Z, Y, 32, BLK), F32),
        compiler_params=small,
        name="final",
    )(place, arrived)
    return (vectors, affinity.reshape(2, 32, 1, 1, 32, BLK))


def solution(mesh):
    split = Mesh(
        mesh.devices.reshape(mesh.shape["freq"], 8, 4, mesh.shape["col"]),
        ("freq", "row_0", "row_1", "col"),
    )
    placed = (
        P(ROW_COL, "freq", None, None),
        P(),
        P(ROW_COL, "freq", None),
        P(ROW, None, "col", None),
    )
    return jax.shard_map(
        body,
        mesh=split,
        in_specs=placed,
        out_specs=(P(ROW_COL, "freq", None), P(ROW, None, "col", None, "freq", None)),
        check_vma=False,
    )
```

```python
import math

import jax
import jax.numpy as jnp
from jax import lax
from jax.experimental import pallas as pl
from jax.experimental.pallas import tpu as pltpu
from jax.sharding import Mesh
from jax.sharding import PartitionSpec as P

ANG = 128
COMP = 64
COLS = 64
BLK = 128
FREQ_DEV = 2
IMG_DEV = 32
Z = 8
X = 4
Y = 4
PAIR = 2 * BLK
EXTRA = 16
KEPT = 4 * Z
ROWS = X * Y * PAIR
MSG = PAIR + EXTRA
ROW = ("row_0", "row_1")
ROW_COL = ("row_0", "row_1", "col")
F32 = jnp.float32
BF16 = jnp.bfloat16


def make_table(angles, freq_count):
    angle_ids = jnp.arange(angles, dtype=jnp.int32)
    orders = jnp.arange(freq_count, dtype=jnp.int32) + 1
    phase_steps = angle_ids[:, None] * orders[None, :] % angles
    phase_angle = phase_steps.astype(jnp.float32) * (2.0 * math.pi / angles)
    table_scale = 1.0 / math.sqrt(angles)
    return jnp.stack(
        [jnp.cos(phase_angle) * table_scale, -jnp.sin(phase_angle) * table_scale], axis=1
    ).astype(jnp.bfloat16)


def nt_dot(left, right):
    return lax.dot_general(
        left, right, (((1,), (1,)), ((), ())), preferred_element_type=jnp.float32
    )


def lane_signs(shape):
    lanes = lax.broadcasted_iota(jnp.int32, shape, len(shape) - 1)
    return jnp.where(lanes < COMP, -1.0, 1.0).astype(F32)


def swapped(block):
    wide = block.astype(F32)
    return (pltpu.roll(wide, COMP, 1) * lane_signs(wide.shape)).astype(BF16)


def swapped_back(block):
    wide = block.astype(F32)
    return (pltpu.roll(wide, COMP, 1) * -lane_signs(wide.shape)).astype(BF16)


def split_rows(rows):
    high = rows.astype(BF16)
    low = (rows - high.astype(F32)).astype(BF16)
    zeros = jnp.zeros((EXTRA - 4, BLK), BF16)
    return jnp.concatenate([high.astype(F32), low.astype(F32), zeros.astype(F32)], axis=0).astype(
        BF16
    )


def joined_rows(extra):
    total = jnp.sum(extra.astype(F32), axis=0)
    return total[0:2] + total[2:4]


def to_column(row):
    rows = lax.broadcasted_iota(jnp.int32, (BLK, BLK), 0)
    cols = lax.broadcasted_iota(jnp.int32, (BLK, BLK), 1)
    return jnp.sum(jnp.where(rows == cols, row, 0.0), axis=1, keepdims=True)


def load_stack(stack_ref, col_refs):
    for z in range(Z):
        block = col_refs[z][...]
        twice = swapped(block) * jnp.asarray(2.0, BF16)
        stack_ref[z * 2 * PAIR : z * 2 * PAIR + PAIR, :] = block
        stack_ref[z * 2 * PAIR + PAIR : (z + 1) * 2 * PAIR, :] = twice


def prepare(coef_ref, kept_ref, own_ref, msg_ref, wide_ref):
    for q in range(4):
        for b in range(2):
            wide_ref[pl.ds(b * BLK + q, IMG_DEV, stride=4), :] = coef_ref[q * 2 + b].astype(F32)
    own = wide_ref[...].astype(BF16)
    own_ref[...] = own
    for k in range(Y):
        msg_ref[k, :PAIR, :] = own
        msg_ref[k, PAIR:, :] = kept_ref[k]


def cross_kernel(place, rows_ref, mask_ref, *refs):
    col_refs, first_refs = refs[:Z], refs[Z : 2 * Z]
    kern_ref, msg_ref, stack_ref, mask_rows = refs[2 * Z :]
    step = pl.program_id(0)

    @pl.when(step == 0)
    def _():
        load_stack(stack_ref, first_refs)

    mask_rows[...] = mask_ref[0].astype(F32)
    powers = []
    for b in range(2):
        block = rows_ref[0, b * BLK : (b + 1) * BLK, :] * jnp.asarray(1.0 / COMP, BF16)
        left = jnp.concatenate([block, swapped_back(block)], axis=0)
        acc = jnp.zeros((BLK, BLK), F32)
        for z in range(Z):
            base = b * 2 * Z + 2 * ((place[1] - z) & (Z - 1))
            masked = [
                col_refs[z][h * BLK : (h + 1) * BLK, :]
                * mask_rows[pl.ds(base + h, 1), :].astype(BF16)
                for h in range(2)
            ]
            cross = nt_dot(left, jnp.concatenate(masked, axis=0))
            re = cross[:BLK]
            im = cross[BLK:]
            re2 = re * re
            im2 = im * im
            at = z * 2 * PAIR
            kern_ref[step, b, :, at : at + PAIR] = (re2 - im2).astype(BF16)
            kern_ref[step, b, :, at + PAIR : at + 2 * PAIR] = (re * im).astype(BF16)
            mag = re2 + im2
            mag = mag * mag
            acc = acc + mag[:, :BLK] + mag[:, BLK:]
        high = acc.astype(BF16)
        low = (acc - high.astype(F32)).astype(BF16)
        ones = jnp.ones((EXTRA, BLK), BF16)
        powers.append((nt_dot(ones, high) + nt_dot(ones, low))[0:1])
    kernel = kern_ref[step].reshape(PAIR, 2 * Z * PAIR)
    product = jnp.dot(kernel, stack_ref[...], preferred_element_type=F32)
    msg_ref[0, :PAIR, :] = product.astype(BF16)
    msg_ref[0, PAIR:, :] = split_rows(jnp.concatenate(powers, axis=0))


def product_kernel(kern_ref, *refs):
    col_refs = refs[:Z]
    msg_ref, stack_ref, sums_ref = refs[Z:]
    step = pl.program_id(0)

    @pl.when(step == 0)
    def _():
        load_stack(stack_ref, col_refs)
        sums_ref[...] = split_rows(block_sums([ref[...].astype(F32) for ref in col_refs]))

    kernel = kern_ref[step].reshape(PAIR, 2 * Z * PAIR)
    product = jnp.dot(kernel, stack_ref[...], preferred_element_type=F32)
    msg_ref[0, :PAIR, :] = product.astype(BF16)
    msg_ref[0, PAIR:, :] = sums_ref[...]


def block_sums(blocks):
    rows = []
    for b in range(2):
        acc = jnp.zeros((BLK, BLK), F32)
        for block in blocks:
            part = block[b * BLK : (b + 1) * BLK]
            acc = acc + part * part
        rows.append(jnp.sum(acc, axis=0, keepdims=True))
    both = jnp.concatenate(rows + rows + rows + rows, axis=0)
    return (both + pltpu.roll(both, COLS, 1))[0:2]


def first_combine(recv_ref, out_ref, inverse_ref):
    powers = joined_rows(recv_ref[:, PAIR:, :])
    inverse = lax.rsqrt(powers)
    for b in range(2):
        total = jnp.sum(recv_ref[:, b * BLK : (b + 1) * BLK, :].astype(F32), axis=0)
        column = jnp.broadcast_to(to_column(inverse[b : b + 1]), (BLK, BLK))
        inverse_ref[b * BLK : (b + 1) * BLK, :] = column
        out_ref[b * BLK : (b + 1) * BLK, :] = (total * column).astype(BF16)


def second_combine(recv_ref, inverse_ref, scaled_ref, own_ref, msg_ref, *, images):
    means = joined_rows(recv_ref[:, PAIR:, :]) / images
    factor = lax.rsqrt(means[0:1] + means[1:2] + 1e-06)
    total = jnp.sum(recv_ref[:, :PAIR, :].astype(F32), axis=0)
    value = total * inverse_ref[...] * factor
    scaled_ref[...] = value
    own = value.astype(BF16)
    own_ref[...] = own
    extra = split_rows(block_sums([value]))
    for k in range(X * Y):
        msg_ref[k, :PAIR, :] = own
        msg_ref[k, PAIR:, :] = extra


def sums_kernel(recv_ref, out_ref):
    rows = []
    for x in range(X):
        total = jnp.sum(recv_ref[x * Y : (x + 1) * Y].astype(F32), axis=0)
        rows.append(jnp.sum(total, axis=0, keepdims=True))
    total = jnp.concatenate(rows + rows, axis=0)
    for k in range(2 * Z):
        out_ref[k] = total


def pack_kernel(place, rows_ref, *refs):
    col_refs, out_ref = refs[:X], refs[X]
    other = (1 - place[0]) * BLK
    for k in range(X * Y):
        out_ref[k * PAIR : (k + 1) * PAIR, :] = rows_ref[k, :PAIR, :]
    for k in range(2 * X):
        at = ROWS + k * BLK
        source = pl.multiple_of(k % 2 * PAIR + other, BLK)
        out_ref[at : at + BLK, :] = col_refs[k // 2][pl.ds(source, BLK), :]


def gram_kernel(place, mask_ref, rows_ref, sums_ref, scaled_ref, got_ref, *refs, images, freqs):
    col_refs = refs[:X]
    out_ref, vec_ref, mask_rows, factors, scaled_cols = refs[X:]
    step = pl.program_id(0)
    core, me_z, me_y, me_x = place[0], place[1], place[2], place[3]
    mine = pl.multiple_of(core * BLK, BLK)

    @pl.when(step == 0)
    def _():
        for c in range(2):
            total = sums_ref[c]
            for z in range(1, Z):
                total = total + sums_ref[2 * z + c]
            factors[c] = lax.rsqrt(total / images + 1e-06)
        mine_factor = factors[core, pl.ds(me_x, 1), :]
        vec_ref[core] = (scaled_ref[pl.ds(mine, BLK), :] * mine_factor).astype(BF16)
        at = pl.multiple_of(((me_x * Y + me_y) * 2 + core) * BLK, BLK)
        block = got_ref[pl.ds(at, BLK), :].astype(F32)
        vec_ref[1 - core] = (block * factors[1 - core, pl.ds(me_x, 1), :]).astype(BF16)
        for r in range(X):
            from_x = (me_x - r) & (X - 1)
            for p in range(2):
                scale = factors[core if p == 0 else 1 - core, pl.ds(from_x, 1), :]
                scale = scale * scale
                for h in range(2):
                    if h == 0:
                        source = pl.multiple_of(p * PAIR + mine, BLK)
                        block = col_refs[r][pl.ds(source, BLK), :]
                    else:
                        far_at = ROWS + (2 * r + 1 - p) * BLK
                        block = got_ref[far_at : far_at + BLK, :]
                    block = (block.astype(F32) * scale).astype(BF16)
                    scaled_cols[2 * r + p, h * BLK : (h + 1) * BLK, :] = block
                    scaled_cols[2 * r + p, (2 + h) * BLK : (3 + h) * BLK, :] = swapped(block)

    mask_rows[...] = mask_ref[0].astype(F32)
    total = jnp.zeros((PAIR, PAIR), F32)
    for r in range(X):
        source = ((me_x - r) & (X - 1)) * Y + step
        at = pl.multiple_of(source * PAIR, PAIR)
        for p in range(2):
            rows = rows_ref[source, :PAIR, :] if p == 0 else got_ref[pl.ds(at, PAIR), :]
            gram = nt_dot(rows, scaled_cols[2 * r + p])
            total = total + gram[:, :PAIR] * gram[:, :PAIR] + gram[:, PAIR:] * gram[:, PAIR:]
    for b in range(2):
        for h in range(2):
            slot = core if h == 0 else 1 - core
            where = (me_z + 2 * me_x + slot) & (Z - 1)
            mask = mask_rows[pl.ds(b * 2 * Z + 2 * where + core, 1), :]
            value = total[b * BLK : (b + 1) * BLK, h * BLK : (h + 1) * BLK]
            value = (value * (mask * (1.0 / (COLS * freqs)))).astype(BF16)
            for x in range(X):
                out_ref[x, 0, b, slot] = value[x * 32 : (x + 1) * 32]


def final_spread(place, tiles_ref, out_ref):
    for x in range(X):
        for h in range(2):
            where = (place[1] + 2 * x + h) & (Z - 1)
            for y in range(Y):
                out_ref[0, where, y] = tiles_ref[x * Y + y, 0, h].astype(F32)


def exchange(pieces, axes):
    return lax.all_to_all(pieces, axes, 0, 0, tiled=True)


def shifted(block, by):
    size = lax.axis_size("row_0")
    return lax.ppermute(block, "row_0", [(i, (i + by) % size) for i in range(size)])


def near(block):
    return [block] + [shifted(block, by) for by in (1, 2, -2, -1)]


def far(blocks):
    own, one, two, back_two, back_one = blocks
    three = shifted(two, 1)
    back_three = shifted(back_two, -1)
    four = shifted(two, 2)
    return [own, one, two, three, four, back_three, back_two, back_one]


def last_columns(block):
    found = []
    for r in range(X):
        pairs = []
        for x in range(X):
            for z in range(Z):
                for c in range(2):
                    to_x = (x + r) % X
                    to_z = (z - 2 * to_x - c) % Z
                    pairs.append(((x * Z + z) * 2 + c, (to_x * Z + to_z) * 2 + c))
        found.append(lax.ppermute(block, ("freq", "row_0", "col"), pairs))
    return found


def body(spectra, basis, start_vectors, pattern):
    group_devices = lax.axis_size("freq")
    images = BLK * lax.axis_size(ROW_COL)
    freq_total = FREQ_DEV * group_devices
    col = lax.axis_index("col")
    places = [col] + [lax.axis_index(name) for name in ("row_0", "row_1", "freq")]
    place = jnp.stack(places).astype(jnp.int32)
    dft_table = make_table(ANG, freq_total)
    angular = lax.dot_general(
        dft_table, spectra[:, 0], (((0,), (1,)), ((), ())), preferred_element_type=jnp.float32
    ).astype(jnp.bfloat16)
    radial = lax.dot_general(
        angular, basis, (((3,), (0,)), ((), ())), preferred_element_type=jnp.float32
    ).astype(jnp.bfloat16)
    coef_local = jnp.transpose(radial, (1, 2, 0, 3)).reshape(freq_total, IMG_DEV, 2 * COMP)
    start = jnp.transpose(start_vectors, (1, 0, 2))
    here = jnp.where(col == 0, start[0], start[1])
    there = jnp.where(col == 0, start[1], start[0])
    there = lax.ppermute(there, "col", [(0, 1), (1, 0)])
    start = jnp.concatenate(
        [jnp.where(col == 0, here, there), jnp.where(col == 0, there, here)], axis=0
    )
    flags = pattern.reshape(2, Z, Y).astype(BF16)
    flags = jnp.broadcast_to(flags.reshape(2 * Z * Y, 1), (2 * Z * Y, BLK))
    flags_other = lax.ppermute(flags, "col", [(0, 1), (1, 0)])
    regrouped = exchange(coef_local, ("freq", "col"))
    both = [jnp.where(col == 0, flags, flags_other), jnp.where(col == 0, flags_other, flags)]
    kept = jnp.stack([flag.reshape(2, Z, Y, BLK) for flag in both], axis=2)
    kept = jnp.transpose(kept, (3, 0, 1, 2, 4)).reshape(Y, KEPT, BLK)
    first = near(start)
    regrouped, kept = lax.optimization_barrier((regrouped, kept))
    own_shape = (PAIR, BLK)
    own_type = jax.ShapeDtypeStruct(own_shape, BF16)
    msg_shape = jax.ShapeDtypeStruct((Y, MSG, BLK), BF16)
    big = pltpu.CompilerParams(vmem_limit_bytes=24 << 20)
    small = pltpu.CompilerParams(vmem_limit_bytes=6 << 20)
    own, to_y = pl.pallas_call(
        prepare,
        out_shape=[own_type, jax.ShapeDtypeStruct((Y, PAIR + KEPT, BLK), BF16)],
        scratch_shapes=[pltpu.VMEM(own_shape, F32)],
        compiler_params=small,
        name="prepare",
    )(regrouped, kept)
    rows = exchange(to_y, "row_1")
    cols = far(near(own))
    first = far(first)

    row_spec = pl.BlockSpec((1, PAIR, BLK), lambda i, p: (i, 0, 0))
    mask_spec = pl.BlockSpec((1, KEPT, BLK), lambda i, p: (i, PAIR // KEPT, 0))
    held = pl.BlockSpec(memory_space=pltpu.VMEM)
    stack = pltpu.VMEM((2 * Z * PAIR, BLK), BF16)
    mask_rows = pltpu.VMEM((KEPT, BLK), F32)
    kernels, partial = pl.pallas_call(
        cross_kernel,
        grid_spec=pltpu.PrefetchScalarGridSpec(
            num_scalar_prefetch=1,
            grid=(Y,),
            in_specs=[row_spec, mask_spec] + [held] * (2 * Z),
            out_specs=[held, pl.BlockSpec((1, MSG, BLK), lambda i, p: (i, 0, 0))],
            scratch_shapes=[stack, mask_rows],
        ),
        out_shape=[jax.ShapeDtypeStruct((Y, 2, BLK, 2 * Z * PAIR), BF16), msg_shape],
        compiler_params=big,
        name="cross",
    )(place, rows, rows, *cols, *first)
    got = exchange(partial, "row_1")
    own, inverse = pl.pallas_call(
        first_combine,
        out_shape=[own_type, jax.ShapeDtypeStruct(own_shape, F32)],
        compiler_params=small,
        name="combine_one",
    )(got)
    cols = far(near(own))
    partial = pl.pallas_call(
        product_kernel,
        grid=(Y,),
        in_specs=[held] * (1 + Z),
        out_specs=pl.BlockSpec((1, MSG, BLK), lambda i: (i, 0, 0)),
        out_shape=msg_shape,
        scratch_shapes=[stack, pltpu.VMEM((EXTRA, BLK), BF16)],
        compiler_params=big,
        name="product",
    )(kernels, *cols)
    got = exchange(partial, "row_1")
    scaled, own, to_xy = pl.pallas_call(
        lambda *refs: second_combine(*refs, images=images),
        out_shape=[
            jax.ShapeDtypeStruct(own_shape, F32),
            own_type,
            jax.ShapeDtypeStruct((X * Y, MSG, BLK), BF16),
        ],
        compiler_params=small,
        name="combine_two",
    )(got, inverse)
    last_rows = exchange(to_xy, ("freq", "row_1"))
    partner = lax.ppermute(own, "col", [(0, 1), (1, 0)])
    cols = last_columns(jnp.concatenate([own, partner], axis=0))
    sums = pl.pallas_call(
        sums_kernel,
        grid=(1,),
        in_specs=[pl.BlockSpec((X * Y, EXTRA, BLK), lambda i: (0, PAIR // EXTRA, 0))],
        out_specs=pl.BlockSpec((2 * Z, 8, BLK), lambda i: (0, 0, 0)),
        out_shape=jax.ShapeDtypeStruct((2 * Z, 8, BLK), F32),
        compiler_params=small,
        name="sums",
    )(last_rows)
    sums = exchange(sums, ("row_0", "col"))
    sums, cols = lax.optimization_barrier((sums, cols))
    packed = pl.pallas_call(
        pack_kernel,
        in_specs=[pl.BlockSpec(memory_space=pltpu.SMEM)] + [held] * (1 + X),
        out_specs=held,
        out_shape=jax.ShapeDtypeStruct((ROWS + 2 * X * BLK, BLK), BF16),
        compiler_params=small,
        name="pack",
    )(place, last_rows, *cols)
    packed = lax.ppermute(packed, "col", [(0, 1), (1, 0)])
    tiles, vectors = pl.pallas_call(
        lambda *refs: gram_kernel(*refs, images=images, freqs=freq_total),
        grid_spec=pltpu.PrefetchScalarGridSpec(
            num_scalar_prefetch=1,
            grid=(Y,),
            in_specs=[mask_spec] + [held] * (4 + X),
            out_specs=[
                pl.BlockSpec((X, 1, 2, 2, 32, BLK), lambda i, p: (0, i, 0, 0, 0, 0)),
                pl.BlockSpec((FREQ_DEV, BLK, BLK), lambda i, p: (0, 0, 0)),
            ],
            scratch_shapes=[
                mask_rows,
                pltpu.VMEM((2, 8, BLK), F32),
                pltpu.VMEM((2 * X, 2 * PAIR, BLK), BF16),
            ],
        ),
        out_shape=[
            jax.ShapeDtypeStruct((X, Y, 2, 2, 32, BLK), BF16),
            jax.ShapeDtypeStruct((FREQ_DEV, BLK, BLK), BF16),
        ],
        compiler_params=big,
        name="gram",
    )(place, rows, last_rows, sums, scaled, packed, *cols)
    arrived = exchange(tiles.reshape(X * Y, 2, 2, 32, BLK), ("freq", "row_1"))
    arrived, vectors = lax.optimization_barrier((arrived, vectors))
    vectors = jnp.transpose(vectors, (1, 0, 2))
    affinity = pl.pallas_call(
        final_spread,
        grid_spec=pltpu.PrefetchScalarGridSpec(
            num_scalar_prefetch=1,
            grid=(2,),
            in_specs=[pl.BlockSpec((X * Y, 1, 2, 32, BLK), lambda b, p: (0, b, 0, 0, 0))],
            out_specs=pl.BlockSpec((1, Z, Y, 32, BLK), lambda b, p: (b, 0, 0, 0, 0)),
        ),
        out_shape=jax.ShapeDtypeStruct((2, Z, Y, 32, BLK), F32),
        compiler_params=small,
        name="final",
    )(place, arrived)
    return (vectors, affinity.reshape(2, 32, 1, 1, 32, BLK))


def solution(mesh):
    split = Mesh(
        mesh.devices.reshape(mesh.shape["freq"], 8, 4, mesh.shape["col"]),
        ("freq", "row_0", "row_1", "col"),
    )
    placed = (
        P(ROW_COL, "freq", None, None),
        P(),
        P(ROW_COL, "freq", None),
        P(ROW, None, "col", None),
    )
    return jax.shard_map(
        body,
        mesh=split,
        in_specs=placed,
        out_specs=(P(ROW_COL, "freq", None), P(ROW, None, "col", None, "freq", None)),
        check_vma=False,
    )
```

```python
import math

import jax
import jax.numpy as jnp
from jax import lax
from jax.experimental import pallas as pl
from jax.experimental.pallas import tpu as pltpu
from jax.sharding import Mesh
from jax.sharding import PartitionSpec as P

ANG = 128
COMP = 64
COLS = 64
BLK = 128
FREQ_DEV = 2
IMG_DEV = 32
Z = 8
X = 4
Y = 4
PAIR = 2 * BLK
EXTRA = 16
KEPT = 4 * Z
ROWS = X * Y * PAIR
MSG = PAIR + EXTRA
ROW = ("row_0", "row_1")
ROW_COL = ("row_0", "row_1", "col")
F32 = jnp.float32
BF16 = jnp.bfloat16


def make_table(angles, freq_count):
    angle_ids = jnp.arange(angles, dtype=jnp.int32)
    orders = jnp.arange(freq_count, dtype=jnp.int32) + 1
    phase_steps = angle_ids[:, None] * orders[None, :] % angles
    phase_angle = phase_steps.astype(jnp.float32) * (2.0 * math.pi / angles)
    table_scale = 1.0 / math.sqrt(angles)
    return jnp.stack(
        [jnp.cos(phase_angle) * table_scale, -jnp.sin(phase_angle) * table_scale], axis=1
    ).astype(jnp.bfloat16)


def nt_dot(left, right):
    return lax.dot_general(
        left, right, (((1,), (1,)), ((), ())), preferred_element_type=jnp.float32
    )


def lane_signs(shape):
    lanes = lax.broadcasted_iota(jnp.int32, shape, len(shape) - 1)
    return jnp.where(lanes < COMP, -1.0, 1.0).astype(F32)


def swapped(block):
    wide = block.astype(F32)
    return (pltpu.roll(wide, COMP, 1) * lane_signs(wide.shape)).astype(BF16)


def swapped_back(block):
    wide = block.astype(F32)
    return (pltpu.roll(wide, COMP, 1) * -lane_signs(wide.shape)).astype(BF16)


def split_rows(rows):
    high = rows.astype(BF16)
    low = (rows - high.astype(F32)).astype(BF16)
    zeros = jnp.zeros((EXTRA - 4, BLK), BF16)
    return jnp.concatenate([high.astype(F32), low.astype(F32), zeros.astype(F32)], axis=0).astype(
        BF16
    )


def joined_rows(extra):
    total = jnp.sum(extra.astype(F32), axis=0)
    return total[0:2] + total[2:4]


def to_column(row):
    rows = lax.broadcasted_iota(jnp.int32, (BLK, BLK), 0)
    cols = lax.broadcasted_iota(jnp.int32, (BLK, BLK), 1)
    return jnp.sum(jnp.where(rows == cols, row, 0.0), axis=1, keepdims=True)


def load_stack(stack_ref, col_refs, offset):
    for z in range(Z):
        block = col_refs[z][offset : offset + PAIR, :]
        twice = swapped(block) * jnp.asarray(2.0, BF16)
        stack_ref[z * 2 * PAIR : z * 2 * PAIR + PAIR, :] = block
        stack_ref[z * 2 * PAIR + PAIR : (z + 1) * 2 * PAIR, :] = twice


def prepare(coef_ref, kept_ref, start_ref, own_ref, msg_ref, wide_ref):
    for q in range(4):
        for b in range(2):
            wide_ref[pl.ds(b * BLK + q, IMG_DEV, stride=4), :] = coef_ref[q * 2 + b].astype(F32)
    own = wide_ref[...].astype(BF16)
    own_ref[:PAIR, :] = own
    own_ref[PAIR:, :] = start_ref[...]
    for k in range(Y):
        msg_ref[k, :PAIR, :] = own
        msg_ref[k, PAIR:, :] = kept_ref[k]


def cross_kernel(place, rows_ref, mask_ref, *refs):
    col_refs = refs[:Z]
    kern_ref, msg_ref, stack_ref, mask_rows = refs[Z:]
    step = pl.program_id(0)

    @pl.when(step == 0)
    def _():
        load_stack(stack_ref, col_refs, PAIR)

    mask_rows[...] = mask_ref[0].astype(F32)
    powers = []
    for b in range(2):
        block = rows_ref[0, b * BLK : (b + 1) * BLK, :] * jnp.asarray(1.0 / COMP, BF16)
        left = jnp.concatenate([block, swapped_back(block)], axis=0)
        acc = jnp.zeros((BLK, BLK), F32)
        for z in range(Z):
            base = b * 2 * Z + 2 * ((place[1] - z) & (Z - 1))
            masked = [
                col_refs[z][h * BLK : (h + 1) * BLK, :]
                * mask_rows[pl.ds(base + h, 1), :].astype(BF16)
                for h in range(2)
            ]
            cross = nt_dot(left, jnp.concatenate(masked, axis=0))
            re = cross[:BLK]
            im = cross[BLK:]
            re2 = re * re
            im2 = im * im
            at = z * 2 * PAIR
            kern_ref[step, b, :, at : at + PAIR] = (re2 - im2).astype(BF16)
            kern_ref[step, b, :, at + PAIR : at + 2 * PAIR] = (re * im).astype(BF16)
            mag = re2 + im2
            mag = mag * mag
            acc = acc + mag[:, :BLK] + mag[:, BLK:]
        high = acc.astype(BF16)
        low = (acc - high.astype(F32)).astype(BF16)
        ones = jnp.ones((EXTRA, BLK), BF16)
        powers.append((nt_dot(ones, high) + nt_dot(ones, low))[0:1])
    kernel = kern_ref[step].reshape(PAIR, 2 * Z * PAIR)
    product = jnp.dot(kernel, stack_ref[...], preferred_element_type=F32)
    msg_ref[0, :PAIR, :] = product.astype(BF16)
    msg_ref[0, PAIR:, :] = split_rows(jnp.concatenate(powers, axis=0))


def product_kernel(kern_ref, *refs):
    col_refs = refs[:Z]
    msg_ref, stack_ref, sums_ref = refs[Z:]
    step = pl.program_id(0)

    @pl.when(step == 0)
    def _():
        load_stack(stack_ref, col_refs, 0)
        sums_ref[...] = split_rows(block_sums([ref[...].astype(F32) for ref in col_refs]))

    kernel = kern_ref[step].reshape(PAIR, 2 * Z * PAIR)
    product = jnp.dot(kernel, stack_ref[...], preferred_element_type=F32)
    msg_ref[0, :PAIR, :] = product.astype(BF16)
    msg_ref[0, PAIR:, :] = sums_ref[...]


def block_sums(blocks):
    rows = []
    for b in range(2):
        acc = jnp.zeros((BLK, BLK), F32)
        for block in blocks:
            part = block[b * BLK : (b + 1) * BLK]
            acc = acc + part * part
        rows.append(jnp.sum(acc, axis=0, keepdims=True))
    both = jnp.concatenate(rows + rows + rows + rows, axis=0)
    return (both + pltpu.roll(both, COLS, 1))[0:2]


def first_combine(recv_ref, out_ref, inverse_ref):
    powers = joined_rows(recv_ref[:, PAIR:, :])
    inverse = lax.rsqrt(powers)
    for b in range(2):
        total = jnp.sum(recv_ref[:, b * BLK : (b + 1) * BLK, :].astype(F32), axis=0)
        column = jnp.broadcast_to(to_column(inverse[b : b + 1]), (BLK, BLK))
        inverse_ref[b * BLK : (b + 1) * BLK, :] = column
        out_ref[b * BLK : (b + 1) * BLK, :] = (total * column).astype(BF16)


def second_combine(recv_ref, inverse_ref, scaled_ref, own_ref, msg_ref, *, images):
    means = joined_rows(recv_ref[:, PAIR:, :]) / images
    factor = lax.rsqrt(means[0:1] + means[1:2] + 1e-06)
    total = jnp.sum(recv_ref[:, :PAIR, :].astype(F32), axis=0)
    value = total * inverse_ref[...] * factor
    scaled_ref[...] = value
    own = value.astype(BF16)
    own_ref[...] = own
    extra = split_rows(block_sums([value]))
    for k in range(X * Y):
        msg_ref[k, :PAIR, :] = own
        msg_ref[k, PAIR:, :] = extra


def sums_kernel(recv_ref, out_ref):
    rows = []
    for x in range(X):
        total = jnp.sum(recv_ref[x * Y : (x + 1) * Y].astype(F32), axis=0)
        rows.append(jnp.sum(total, axis=0, keepdims=True))
    total = jnp.concatenate(rows + rows, axis=0)
    for k in range(2 * Z):
        out_ref[k] = total


def pack_kernel(place, rows_ref, *refs):
    col_refs, out_ref = refs[:X], refs[X]
    other = (1 - place[0]) * BLK
    for k in range(X * Y):
        out_ref[k * PAIR : (k + 1) * PAIR, :] = rows_ref[k, :PAIR, :]
    for k in range(2 * X):
        at = ROWS + k * BLK
        source = pl.multiple_of(k % 2 * PAIR + other, BLK)
        out_ref[at : at + BLK, :] = col_refs[k // 2][pl.ds(source, BLK), :]


def gram_kernel(place, mask_ref, rows_ref, sums_ref, scaled_ref, got_ref, *refs, images, freqs):
    col_refs = refs[:X]
    out_ref, vec_ref, mask_rows, factors, scaled_cols = refs[X:]
    step = pl.program_id(0)
    core, me_z, me_y, me_x = place[0], place[1], place[2], place[3]
    mine = pl.multiple_of(core * BLK, BLK)

    @pl.when(step == 0)
    def _():
        for c in range(2):
            total = sums_ref[c]
            for z in range(1, Z):
                total = total + sums_ref[2 * z + c]
            factors[c] = lax.rsqrt(total / images + 1e-06)
        mine_factor = factors[core, pl.ds(me_x, 1), :]
        vec_ref[core] = (scaled_ref[pl.ds(mine, BLK), :] * mine_factor).astype(BF16)
        at = pl.multiple_of(((me_x * Y + me_y) * 2 + core) * BLK, BLK)
        block = got_ref[pl.ds(at, BLK), :].astype(F32)
        vec_ref[1 - core] = (block * factors[1 - core, pl.ds(me_x, 1), :]).astype(BF16)
        for r in range(X):
            from_x = (me_x - r) & (X - 1)
            for p in range(2):
                scale = factors[core if p == 0 else 1 - core, pl.ds(from_x, 1), :]
                scale = scale * scale
                for h in range(2):
                    if h == 0:
                        source = pl.multiple_of(p * PAIR + mine, BLK)
                        block = col_refs[r][pl.ds(source, BLK), :]
                    else:
                        far_at = ROWS + (2 * r + 1 - p) * BLK
                        block = got_ref[far_at : far_at + BLK, :]
                    block = (block.astype(F32) * scale).astype(BF16)
                    scaled_cols[2 * r + p, h * BLK : (h + 1) * BLK, :] = block
                    scaled_cols[2 * r + p, (2 + h) * BLK : (3 + h) * BLK, :] = swapped(block)

    mask_rows[...] = mask_ref[0].astype(F32)
    total = jnp.zeros((PAIR, PAIR), F32)
    for r in range(X):
        source = ((me_x - r) & (X - 1)) * Y + step
        at = pl.multiple_of(source * PAIR, PAIR)
        for p in range(2):
            rows = rows_ref[source, :PAIR, :] if p == 0 else got_ref[pl.ds(at, PAIR), :]
            gram = nt_dot(rows, scaled_cols[2 * r + p])
            total = total + gram[:, :PAIR] * gram[:, :PAIR] + gram[:, PAIR:] * gram[:, PAIR:]
    for b in range(2):
        for h in range(2):
            slot = core if h == 0 else 1 - core
            where = (me_z + 2 * me_x + slot) & (Z - 1)
            mask = mask_rows[pl.ds(b * 2 * Z + 2 * where + core, 1), :]
            value = total[b * BLK : (b + 1) * BLK, h * BLK : (h + 1) * BLK]
            value = (value * (mask * (1.0 / (COLS * freqs)))).astype(BF16)
            for x in range(X):
                out_ref[x, 0, b, slot] = value[x * 32 : (x + 1) * 32]


def final_spread(place, tiles_ref, out_ref):
    for x in range(X):
        for h in range(2):
            where = (place[1] + 2 * x + h) & (Z - 1)
            for y in range(Y):
                out_ref[0, where, y] = tiles_ref[x * Y + y, 0, h].astype(F32)


def exchange(pieces, axes):
    return lax.all_to_all(pieces, axes, 0, 0, tiled=True)


def shifted(block, by):
    size = lax.axis_size("row_0")
    return lax.ppermute(block, "row_0", [(i, (i + by) % size) for i in range(size)])


def near(block):
    return [block] + [shifted(block, by) for by in (1, 2, -2, -1)]


def far(blocks):
    own, one, two, back_two, back_one = blocks
    three = shifted(two, 1)
    back_three = shifted(back_two, -1)
    four = shifted(two, 2)
    return [own, one, two, three, four, back_three, back_two, back_one]


def last_columns(block):
    found = []
    for r in range(X):
        pairs = []
        for x in range(X):
            for z in range(Z):
                for c in range(2):
                    to_x = (x + r) % X
                    to_z = (z - 2 * to_x - c) % Z
                    pairs.append(((x * Z + z) * 2 + c, (to_x * Z + to_z) * 2 + c))
        found.append(lax.ppermute(block, ("freq", "row_0", "col"), pairs))
    return found


def body(spectra, basis, start_vectors, pattern):
    group_devices = lax.axis_size("freq")
    images = BLK * lax.axis_size(ROW_COL)
    freq_total = FREQ_DEV * group_devices
    col = lax.axis_index("col")
    places = [col] + [lax.axis_index(name) for name in ("row_0", "row_1", "freq")]
    place = jnp.stack(places).astype(jnp.int32)
    dft_table = make_table(ANG, freq_total)
    angular = lax.dot_general(
        dft_table, spectra[:, 0], (((0,), (1,)), ((), ())), preferred_element_type=jnp.float32
    ).astype(jnp.bfloat16)
    radial = lax.dot_general(
        angular, basis, (((3,), (0,)), ((), ())), preferred_element_type=jnp.float32
    ).astype(jnp.bfloat16)
    coef_local = jnp.transpose(radial, (1, 2, 0, 3)).reshape(freq_total, IMG_DEV, 2 * COMP)
    start = jnp.transpose(start_vectors, (1, 0, 2))
    here = jnp.where(col == 0, start[0], start[1])
    there = jnp.where(col == 0, start[1], start[0])
    there = lax.ppermute(there, "col", [(0, 1), (1, 0)])
    start = jnp.concatenate(
        [jnp.where(col == 0, here, there), jnp.where(col == 0, there, here)], axis=0
    )
    flags = pattern.reshape(2, Z, Y).astype(BF16)
    flags = jnp.broadcast_to(flags.reshape(2 * Z * Y, 1), (2 * Z * Y, BLK))
    flags_other = lax.ppermute(flags, "col", [(0, 1), (1, 0)])
    regrouped = exchange(coef_local, ("freq", "col"))
    both = [jnp.where(col == 0, flags, flags_other), jnp.where(col == 0, flags_other, flags)]
    kept = jnp.stack([flag.reshape(2, Z, Y, BLK) for flag in both], axis=2)
    kept = jnp.transpose(kept, (3, 0, 1, 2, 4)).reshape(Y, KEPT, BLK)
    regrouped, kept, start = lax.optimization_barrier((regrouped, kept, start))
    own_shape = (PAIR, BLK)
    own_type = jax.ShapeDtypeStruct(own_shape, BF16)
    msg_shape = jax.ShapeDtypeStruct((Y, MSG, BLK), BF16)
    big = pltpu.CompilerParams(vmem_limit_bytes=24 << 20)
    small = pltpu.CompilerParams(vmem_limit_bytes=6 << 20)
    own, to_y = pl.pallas_call(
        prepare,
        out_shape=[
            jax.ShapeDtypeStruct((2 * PAIR, BLK), BF16),
            jax.ShapeDtypeStruct((Y, PAIR + KEPT, BLK), BF16),
        ],
        scratch_shapes=[pltpu.VMEM(own_shape, F32)],
        compiler_params=small,
        name="prepare",
    )(regrouped, kept, start)
    rows = exchange(to_y, "row_1")
    cols = far(near(own))

    row_spec = pl.BlockSpec((1, PAIR, BLK), lambda i, p: (i, 0, 0))
    mask_spec = pl.BlockSpec((1, KEPT, BLK), lambda i, p: (i, PAIR // KEPT, 0))
    held = pl.BlockSpec(memory_space=pltpu.VMEM)
    stack = pltpu.VMEM((2 * Z * PAIR, BLK), BF16)
    mask_rows = pltpu.VMEM((KEPT, BLK), F32)
    kernels, partial = pl.pallas_call(
        cross_kernel,
        grid_spec=pltpu.PrefetchScalarGridSpec(
            num_scalar_prefetch=1,
            grid=(Y,),
            in_specs=[row_spec, mask_spec] + [held] * Z,
            out_specs=[held, pl.BlockSpec((1, MSG, BLK), lambda i, p: (i, 0, 0))],
            scratch_shapes=[stack, mask_rows],
        ),
        out_shape=[jax.ShapeDtypeStruct((Y, 2, BLK, 2 * Z * PAIR), BF16), msg_shape],
        compiler_params=big,
        name="cross",
    )(place, rows, rows, *cols)
    got = exchange(partial, "row_1")
    own, inverse = pl.pallas_call(
        first_combine,
        out_shape=[own_type, jax.ShapeDtypeStruct(own_shape, F32)],
        compiler_params=small,
        name="combine_one",
    )(got)
    cols = far(near(own))
    partial = pl.pallas_call(
        product_kernel,
        grid=(Y,),
        in_specs=[held] * (1 + Z),
        out_specs=pl.BlockSpec((1, MSG, BLK), lambda i: (i, 0, 0)),
        out_shape=msg_shape,
        scratch_shapes=[stack, pltpu.VMEM((EXTRA, BLK), BF16)],
        compiler_params=big,
        name="product",
    )(kernels, *cols)
    got = exchange(partial, "row_1")
    scaled, own, to_xy = pl.pallas_call(
        lambda *refs: second_combine(*refs, images=images),
        out_shape=[
            jax.ShapeDtypeStruct(own_shape, F32),
            own_type,
            jax.ShapeDtypeStruct((X * Y, MSG, BLK), BF16),
        ],
        compiler_params=small,
        name="combine_two",
    )(got, inverse)
    last_rows = exchange(to_xy, ("freq", "row_1"))
    partner = lax.ppermute(own, "col", [(0, 1), (1, 0)])
    cols = last_columns(jnp.concatenate([own, partner], axis=0))
    sums = pl.pallas_call(
        sums_kernel,
        grid=(1,),
        in_specs=[pl.BlockSpec((X * Y, EXTRA, BLK), lambda i: (0, PAIR // EXTRA, 0))],
        out_specs=pl.BlockSpec((2 * Z, 8, BLK), lambda i: (0, 0, 0)),
        out_shape=jax.ShapeDtypeStruct((2 * Z, 8, BLK), F32),
        compiler_params=small,
        name="sums",
    )(last_rows)
    sums = exchange(sums, ("row_0", "col"))
    sums, cols = lax.optimization_barrier((sums, cols))
    packed = pl.pallas_call(
        pack_kernel,
        in_specs=[pl.BlockSpec(memory_space=pltpu.SMEM)] + [held] * (1 + X),
        out_specs=held,
        out_shape=jax.ShapeDtypeStruct((ROWS + 2 * X * BLK, BLK), BF16),
        compiler_params=small,
        name="pack",
    )(place, last_rows, *cols)
    packed = lax.ppermute(packed, "col", [(0, 1), (1, 0)])
    tiles, vectors = pl.pallas_call(
        lambda *refs: gram_kernel(*refs, images=images, freqs=freq_total),
        grid_spec=pltpu.PrefetchScalarGridSpec(
            num_scalar_prefetch=1,
            grid=(Y,),
            in_specs=[mask_spec] + [held] * (4 + X),
            out_specs=[
                pl.BlockSpec((X, 1, 2, 2, 32, BLK), lambda i, p: (0, i, 0, 0, 0, 0)),
                pl.BlockSpec((FREQ_DEV, BLK, BLK), lambda i, p: (0, 0, 0)),
            ],
            scratch_shapes=[
                mask_rows,
                pltpu.VMEM((2, 8, BLK), F32),
                pltpu.VMEM((2 * X, 2 * PAIR, BLK), BF16),
            ],
        ),
        out_shape=[
            jax.ShapeDtypeStruct((X, Y, 2, 2, 32, BLK), BF16),
            jax.ShapeDtypeStruct((FREQ_DEV, BLK, BLK), BF16),
        ],
        compiler_params=big,
        name="gram",
    )(place, rows, last_rows, sums, scaled, packed, *cols)
    arrived = exchange(tiles.reshape(X * Y, 2, 2, 32, BLK), ("freq", "row_1"))
    arrived, vectors = lax.optimization_barrier((arrived, vectors))
    vectors = jnp.transpose(vectors, (1, 0, 2))
    affinity = pl.pallas_call(
        final_spread,
        grid_spec=pltpu.PrefetchScalarGridSpec(
            num_scalar_prefetch=1,
            grid=(2,),
            in_specs=[pl.BlockSpec((X * Y, 1, 2, 32, BLK), lambda b, p: (0, b, 0, 0, 0))],
            out_specs=pl.BlockSpec((1, Z, Y, 32, BLK), lambda b, p: (b, 0, 0, 0, 0)),
        ),
        out_shape=jax.ShapeDtypeStruct((2, Z, Y, 32, BLK), F32),
        compiler_params=small,
        name="final",
    )(place, arrived)
    return (vectors, affinity.reshape(2, 32, 1, 1, 32, BLK))


def solution(mesh):
    split = Mesh(
        mesh.devices.reshape(mesh.shape["freq"], 8, 4, mesh.shape["col"]),
        ("freq", "row_0", "row_1", "col"),
    )
    placed = (
        P(ROW_COL, "freq", None, None),
        P(),
        P(ROW_COL, "freq", None),
        P(ROW, None, "col", None),
    )
    return jax.shard_map(
        body,
        mesh=split,
        in_specs=placed,
        out_specs=(P(ROW_COL, "freq", None), P(ROW, None, "col", None, "freq", None)),
        check_vma=False,
    )
```

```python
import math

import jax
import jax.numpy as jnp
from jax import lax
from jax.experimental import pallas as pl
from jax.experimental.pallas import tpu as pltpu
from jax.sharding import Mesh
from jax.sharding import PartitionSpec as P

ANG = 128
COMP = 64
COLS = 64
BLK = 128
FREQ_DEV = 2
IMG_DEV = 32
Z = 8
X = 4
Y = 4
PAIR = 2 * BLK
EXTRA = 16
KEPT = 4 * Z
ROWS = X * Y * PAIR
NEAR = (0, 1, 2, 6, 7)
FAR = (3, 4, 5)
MSG = PAIR + EXTRA
ROW = ("row_0", "row_1")
ROW_COL = ("row_0", "row_1", "col")
F32 = jnp.float32
BF16 = jnp.bfloat16


def make_table(angles, freq_count):
    angle_ids = jnp.arange(angles, dtype=jnp.int32)
    orders = jnp.arange(freq_count, dtype=jnp.int32) + 1
    phase_steps = angle_ids[:, None] * orders[None, :] % angles
    phase_angle = phase_steps.astype(jnp.float32) * (2.0 * math.pi / angles)
    table_scale = 1.0 / math.sqrt(angles)
    return jnp.stack(
        [jnp.cos(phase_angle) * table_scale, -jnp.sin(phase_angle) * table_scale], axis=1
    ).astype(jnp.bfloat16)


def nt_dot(left, right):
    return lax.dot_general(
        left, right, (((1,), (1,)), ((), ())), preferred_element_type=jnp.float32
    )


def lane_signs(shape):
    lanes = lax.broadcasted_iota(jnp.int32, shape, len(shape) - 1)
    return jnp.where(lanes < COMP, -1.0, 1.0).astype(F32)


def swapped(block):
    wide = block.astype(F32)
    return (pltpu.roll(wide, COMP, 1) * lane_signs(wide.shape)).astype(BF16)


def swapped_back(block):
    wide = block.astype(F32)
    return (pltpu.roll(wide, COMP, 1) * -lane_signs(wide.shape)).astype(BF16)


def split_rows(rows):
    high = rows.astype(BF16)
    low = (rows - high.astype(F32)).astype(BF16)
    zeros = jnp.zeros((EXTRA - 4, BLK), BF16)
    return jnp.concatenate([high.astype(F32), low.astype(F32), zeros.astype(F32)], axis=0).astype(
        BF16
    )


def joined_rows(extra):
    total = jnp.sum(extra.astype(F32), axis=0)
    return total[0:2] + total[2:4]


def to_column(row):
    rows = lax.broadcasted_iota(jnp.int32, (BLK, BLK), 0)
    cols = lax.broadcasted_iota(jnp.int32, (BLK, BLK), 1)
    return jnp.sum(jnp.where(rows == cols, row, 0.0), axis=1, keepdims=True)


def load_stack(stack_ref, col_refs, offset):
    for z, ref in enumerate(col_refs):
        block = ref[offset : offset + PAIR, :]
        twice = swapped(block) * jnp.asarray(2.0, BF16)
        stack_ref[z * 2 * PAIR : z * 2 * PAIR + PAIR, :] = block
        stack_ref[z * 2 * PAIR + PAIR : (z + 1) * 2 * PAIR, :] = twice


def prepare(coef_ref, kept_ref, start_ref, own_ref, msg_ref, wide_ref):
    for q in range(4):
        for b in range(2):
            wide_ref[pl.ds(b * BLK + q, IMG_DEV, stride=4), :] = coef_ref[q * 2 + b].astype(F32)
    own = wide_ref[...].astype(BF16)
    own_ref[:PAIR, :] = own
    own_ref[PAIR:, :] = start_ref[...]
    for k in range(Y):
        msg_ref[k, :PAIR, :] = own
        msg_ref[k, PAIR:, :] = kept_ref[k]


def cross_blocks(place, rows_ref, mask_ref, col_refs, shifts, kern_ref, stack_ref, mask_rows):
    step = pl.program_id(0)

    @pl.when(step == 0)
    def _():
        load_stack(stack_ref, col_refs, PAIR)

    mask_rows[...] = mask_ref[0].astype(F32)
    powers = []
    for b in range(2):
        block = rows_ref[0, b * BLK : (b + 1) * BLK, :] * jnp.asarray(1.0 / COMP, BF16)
        left = jnp.concatenate([block, swapped_back(block)], axis=0)
        acc = jnp.zeros((BLK, BLK), F32)
        for k, z in enumerate(shifts):
            base = b * 2 * Z + 2 * ((place[1] - z) & (Z - 1))
            masked = [
                col_refs[k][h * BLK : (h + 1) * BLK, :]
                * mask_rows[pl.ds(base + h, 1), :].astype(BF16)
                for h in range(2)
            ]
            cross = nt_dot(left, jnp.concatenate(masked, axis=0))
            re = cross[:BLK]
            im = cross[BLK:]
            re2 = re * re
            im2 = im * im
            at = k * 2 * PAIR
            kern_ref[step, b, :, at : at + PAIR] = (re2 - im2).astype(BF16)
            kern_ref[step, b, :, at + PAIR : at + 2 * PAIR] = (re * im).astype(BF16)
            mag = re2 + im2
            mag = mag * mag
            acc = acc + mag[:, :BLK] + mag[:, BLK:]
        powers.append(acc)
    kernel = kern_ref[step].reshape(PAIR, 2 * len(shifts) * PAIR)
    product = jnp.dot(kernel, stack_ref[...], preferred_element_type=F32)
    return product, powers


def cross_near(place, rows_ref, mask_ref, *refs):
    count = len(NEAR)
    kern_ref, sum_ref, power_ref, stack_ref, mask_rows = refs[count:]
    product, powers = cross_blocks(
        place, rows_ref, mask_ref, refs[:count], NEAR, kern_ref, stack_ref, mask_rows
    )
    sum_ref[0] = product
    for b in range(2):
        power_ref[0, b] = powers[b]


def cross_far(place, rows_ref, mask_ref, sum_ref, power_ref, *refs):
    count = len(FAR)
    kern_ref, msg_ref, stack_ref, mask_rows = refs[count:]
    product, powers = cross_blocks(
        place, rows_ref, mask_ref, refs[:count], FAR, kern_ref, stack_ref, mask_rows
    )
    msg_ref[0, :PAIR, :] = (product + sum_ref[0]).astype(BF16)
    rows = []
    for b in range(2):
        acc = powers[b] + power_ref[0, b]
        high = acc.astype(BF16)
        low = (acc - high.astype(F32)).astype(BF16)
        ones = jnp.ones((EXTRA, BLK), BF16)
        rows.append((nt_dot(ones, high) + nt_dot(ones, low))[0:1])
    msg_ref[0, PAIR:, :] = split_rows(jnp.concatenate(rows, axis=0))


def product_near(kern_ref, *refs):
    count = len(NEAR)
    sum_ref, stack_ref = refs[count:]
    step = pl.program_id(0)

    @pl.when(step == 0)
    def _():
        load_stack(stack_ref, refs[:count], 0)

    kernel = kern_ref[step].reshape(PAIR, 2 * count * PAIR)
    sum_ref[0] = jnp.dot(kernel, stack_ref[...], preferred_element_type=F32)


def product_far(kern_ref, sum_ref, *refs):
    count = len(FAR)
    msg_ref, stack_ref, sums_ref = refs[Z:]
    step = pl.program_id(0)

    @pl.when(step == 0)
    def _():
        load_stack(stack_ref, refs[:count], 0)
        sums_ref[...] = split_rows(block_sums([ref[...].astype(F32) for ref in refs[:Z]]))

    kernel = kern_ref[step].reshape(PAIR, 2 * count * PAIR)
    product = jnp.dot(kernel, stack_ref[...], preferred_element_type=F32)
    msg_ref[0, :PAIR, :] = (product + sum_ref[0]).astype(BF16)
    msg_ref[0, PAIR:, :] = sums_ref[...]


def block_sums(blocks):
    rows = []
    for b in range(2):
        acc = jnp.zeros((BLK, BLK), F32)
        for block in blocks:
            part = block[b * BLK : (b + 1) * BLK]
            acc = acc + part * part
        rows.append(jnp.sum(acc, axis=0, keepdims=True))
    both = jnp.concatenate(rows + rows + rows + rows, axis=0)
    return (both + pltpu.roll(both, COLS, 1))[0:2]


def first_combine(recv_ref, out_ref, inverse_ref):
    powers = joined_rows(recv_ref[:, PAIR:, :])
    inverse = lax.rsqrt(powers)
    for b in range(2):
        total = jnp.sum(recv_ref[:, b * BLK : (b + 1) * BLK, :].astype(F32), axis=0)
        column = jnp.broadcast_to(to_column(inverse[b : b + 1]), (BLK, BLK))
        inverse_ref[b * BLK : (b + 1) * BLK, :] = column
        out_ref[b * BLK : (b + 1) * BLK, :] = (total * column).astype(BF16)


def second_combine(recv_ref, inverse_ref, scaled_ref, own_ref, msg_ref, *, images):
    means = joined_rows(recv_ref[:, PAIR:, :]) / images
    factor = lax.rsqrt(means[0:1] + means[1:2] + 1e-06)
    total = jnp.sum(recv_ref[:, :PAIR, :].astype(F32), axis=0)
    value = total * inverse_ref[...] * factor
    scaled_ref[...] = value
    own = value.astype(BF16)
    own_ref[...] = own
    extra = split_rows(block_sums([value]))
    for k in range(X * Y):
        msg_ref[k, :PAIR, :] = own
        msg_ref[k, PAIR:, :] = extra


def sums_kernel(recv_ref, out_ref):
    rows = []
    for x in range(X):
        total = jnp.sum(recv_ref[x * Y : (x + 1) * Y].astype(F32), axis=0)
        rows.append(jnp.sum(total, axis=0, keepdims=True))
    total = jnp.concatenate(rows + rows, axis=0)
    for k in range(2 * Z):
        out_ref[k] = total


def pack_kernel(place, rows_ref, *refs):
    col_refs, out_ref = refs[:X], refs[X]
    other = (1 - place[0]) * BLK
    for k in range(X * Y):
        out_ref[k * PAIR : (k + 1) * PAIR, :] = rows_ref[k, :PAIR, :]
    for k in range(2 * X):
        at = ROWS + k * BLK
        source = pl.multiple_of(k % 2 * PAIR + other, BLK)
        out_ref[at : at + BLK, :] = col_refs[k // 2][pl.ds(source, BLK), :]


def gram_kernel(place, mask_ref, rows_ref, sums_ref, scaled_ref, got_ref, *refs, images, freqs):
    col_refs = refs[:X]
    out_ref, vec_ref, mask_rows, factors, scaled_cols = refs[X:]
    step = pl.program_id(0)
    core, me_z, me_y, me_x = place[0], place[1], place[2], place[3]
    mine = pl.multiple_of(core * BLK, BLK)

    @pl.when(step == 0)
    def _():
        for c in range(2):
            total = sums_ref[c]
            for z in range(1, Z):
                total = total + sums_ref[2 * z + c]
            factors[c] = lax.rsqrt(total / images + 1e-06)
        mine_factor = factors[core, pl.ds(me_x, 1), :]
        vec_ref[core] = (scaled_ref[pl.ds(mine, BLK), :] * mine_factor).astype(BF16)
        at = pl.multiple_of(((me_x * Y + me_y) * 2 + core) * BLK, BLK)
        block = got_ref[pl.ds(at, BLK), :].astype(F32)
        vec_ref[1 - core] = (block * factors[1 - core, pl.ds(me_x, 1), :]).astype(BF16)
        for r in range(X):
            from_x = (me_x - r) & (X - 1)
            for p in range(2):
                scale = factors[core if p == 0 else 1 - core, pl.ds(from_x, 1), :]
                scale = scale * scale
                for h in range(2):
                    if h == 0:
                        source = pl.multiple_of(p * PAIR + mine, BLK)
                        block = col_refs[r][pl.ds(source, BLK), :]
                    else:
                        far_at = ROWS + (2 * r + 1 - p) * BLK
                        block = got_ref[far_at : far_at + BLK, :]
                    block = (block.astype(F32) * scale).astype(BF16)
                    scaled_cols[2 * r + p, h * BLK : (h + 1) * BLK, :] = block
                    scaled_cols[2 * r + p, (2 + h) * BLK : (3 + h) * BLK, :] = swapped(block)

    mask_rows[...] = mask_ref[0].astype(F32)
    total = jnp.zeros((PAIR, PAIR), F32)
    for r in range(X):
        source = ((me_x - r) & (X - 1)) * Y + step
        at = pl.multiple_of(source * PAIR, PAIR)
        for p in range(2):
            rows = rows_ref[source, :PAIR, :] if p == 0 else got_ref[pl.ds(at, PAIR), :]
            gram = nt_dot(rows, scaled_cols[2 * r + p])
            total = total + gram[:, :PAIR] * gram[:, :PAIR] + gram[:, PAIR:] * gram[:, PAIR:]
    for b in range(2):
        for h in range(2):
            slot = core if h == 0 else 1 - core
            where = (me_z + 2 * me_x + slot) & (Z - 1)
            mask = mask_rows[pl.ds(b * 2 * Z + 2 * where + core, 1), :]
            value = total[b * BLK : (b + 1) * BLK, h * BLK : (h + 1) * BLK]
            value = (value * (mask * (1.0 / (COLS * freqs)))).astype(BF16)
            for x in range(X):
                out_ref[x, 0, b, slot] = value[x * 32 : (x + 1) * 32]


def final_spread(place, tiles_ref, out_ref):
    for x in range(X):
        for h in range(2):
            where = (place[1] + 2 * x + h) & (Z - 1)
            for y in range(Y):
                out_ref[0, where, y] = tiles_ref[x * Y + y, 0, h].astype(F32)


def exchange(pieces, axes):
    return lax.all_to_all(pieces, axes, 0, 0, tiled=True)


def shifted(block, by):
    size = lax.axis_size("row_0")
    return lax.ppermute(block, "row_0", [(i, (i + by) % size) for i in range(size)])


def near(block):
    return [block] + [shifted(block, by) for by in (1, 2, -2, -1)]


def far(blocks):
    own, one, two, back_two, back_one = blocks
    three = shifted(two, 1)
    back_three = shifted(back_two, -1)
    four = shifted(two, 2)
    return [own, one, two, three, four, back_three, back_two, back_one]


def last_columns(block):
    found = []
    for r in range(X):
        pairs = []
        for x in range(X):
            for z in range(Z):
                for c in range(2):
                    to_x = (x + r) % X
                    to_z = (z - 2 * to_x - c) % Z
                    pairs.append(((x * Z + z) * 2 + c, (to_x * Z + to_z) * 2 + c))
        found.append(lax.ppermute(block, ("freq", "row_0", "col"), pairs))
    return found


def body(spectra, basis, start_vectors, pattern):
    group_devices = lax.axis_size("freq")
    images = BLK * lax.axis_size(ROW_COL)
    freq_total = FREQ_DEV * group_devices
    col = lax.axis_index("col")
    places = [col] + [lax.axis_index(name) for name in ("row_0", "row_1", "freq")]
    place = jnp.stack(places).astype(jnp.int32)
    dft_table = make_table(ANG, freq_total)
    angular = lax.dot_general(
        dft_table, spectra[:, 0], (((0,), (1,)), ((), ())), preferred_element_type=jnp.float32
    ).astype(jnp.bfloat16)
    radial = lax.dot_general(
        angular, basis, (((3,), (0,)), ((), ())), preferred_element_type=jnp.float32
    ).astype(jnp.bfloat16)
    coef_local = jnp.transpose(radial, (1, 2, 0, 3)).reshape(freq_total, IMG_DEV, 2 * COMP)
    coef_local, start_vectors, pattern = lax.optimization_barrier(
        (coef_local, start_vectors, pattern)
    )
    start = jnp.transpose(start_vectors, (1, 0, 2))
    here = jnp.where(col == 0, start[0], start[1])
    there = jnp.where(col == 0, start[1], start[0])
    there = lax.ppermute(there, "col", [(0, 1), (1, 0)])
    start = jnp.concatenate(
        [jnp.where(col == 0, here, there), jnp.where(col == 0, there, here)], axis=0
    )
    flags = pattern.reshape(2, Z, Y).astype(BF16)
    flags = jnp.broadcast_to(flags.reshape(2 * Z * Y, 1), (2 * Z * Y, BLK))
    flags_other = lax.ppermute(flags, "col", [(0, 1), (1, 0)])
    regrouped = exchange(coef_local, ("freq", "col"))
    both = [jnp.where(col == 0, flags, flags_other), jnp.where(col == 0, flags_other, flags)]
    kept = jnp.stack([flag.reshape(2, Z, Y, BLK) for flag in both], axis=2)
    kept = jnp.transpose(kept, (3, 0, 1, 2, 4)).reshape(Y, KEPT, BLK)
    regrouped, kept, start = lax.optimization_barrier((regrouped, kept, start))
    own_shape = (PAIR, BLK)
    own_type = jax.ShapeDtypeStruct(own_shape, BF16)
    msg_shape = jax.ShapeDtypeStruct((Y, MSG, BLK), BF16)
    big = pltpu.CompilerParams(vmem_limit_bytes=24 << 20)
    small = pltpu.CompilerParams(vmem_limit_bytes=6 << 20)
    own, to_y = pl.pallas_call(
        prepare,
        out_shape=[
            jax.ShapeDtypeStruct((2 * PAIR, BLK), BF16),
            jax.ShapeDtypeStruct((Y, PAIR + KEPT, BLK), BF16),
        ],
        scratch_shapes=[pltpu.VMEM(own_shape, F32)],
        compiler_params=small,
        name="prepare",
    )(regrouped, kept, start)
    rows = exchange(to_y, "row_1")
    cols = far(near(own))

    row_spec = pl.BlockSpec((1, PAIR, BLK), lambda i, p: (i, 0, 0))
    mask_spec = pl.BlockSpec((1, KEPT, BLK), lambda i, p: (i, PAIR // KEPT, 0))
    held = pl.BlockSpec(memory_space=pltpu.VMEM)
    mask_rows = pltpu.VMEM((KEPT, BLK), F32)
    near_stack = pltpu.VMEM((2 * len(NEAR) * PAIR, BLK), BF16)
    far_stack = pltpu.VMEM((2 * len(FAR) * PAIR, BLK), BF16)
    near_kern = jax.ShapeDtypeStruct((Y, 2, BLK, 2 * len(NEAR) * PAIR), BF16)
    far_kern = jax.ShapeDtypeStruct((Y, 2, BLK, 2 * len(FAR) * PAIR), BF16)
    sum_shape = jax.ShapeDtypeStruct((Y, PAIR, BLK), F32)
    power_shape = jax.ShapeDtypeStruct((Y, 2, BLK, BLK), F32)
    msg_spec = pl.BlockSpec((1, MSG, BLK), lambda i, p: (i, 0, 0))
    power_spec = pl.BlockSpec((1, 2, BLK, BLK), lambda i, p: (i, 0, 0, 0))

    def work(count, both):
        return pl.CostEstimate(
            flops=count * (70_000_000 if both else 35_000_000),
            bytes_accessed=count * 1_500_000,
            transcendentals=0,
        )

    near_kernels, near_sum, near_power = pl.pallas_call(
        cross_near,
        grid_spec=pltpu.PrefetchScalarGridSpec(
            num_scalar_prefetch=1,
            grid=(Y,),
            in_specs=[row_spec, mask_spec] + [held] * len(NEAR),
            out_specs=[held, row_spec, power_spec],
            scratch_shapes=[near_stack, mask_rows],
        ),
        out_shape=[near_kern, sum_shape, power_shape],
        compiler_params=big,
        cost_estimate=work(len(NEAR), True),
        name="cross_near",
    )(place, rows, rows, *[cols[z] for z in NEAR])
    far_kernels, partial = pl.pallas_call(
        cross_far,
        grid_spec=pltpu.PrefetchScalarGridSpec(
            num_scalar_prefetch=1,
            grid=(Y,),
            in_specs=[row_spec, mask_spec, row_spec, power_spec] + [held] * len(FAR),
            out_specs=[held, msg_spec],
            scratch_shapes=[far_stack, mask_rows],
        ),
        out_shape=[far_kern, msg_shape],
        compiler_params=big,
        cost_estimate=work(len(FAR), True),
        name="cross_far",
    )(place, rows, rows, near_sum, near_power, *[cols[z] for z in FAR])
    got = exchange(partial, "row_1")
    own, inverse = pl.pallas_call(
        first_combine,
        out_shape=[own_type, jax.ShapeDtypeStruct(own_shape, F32)],
        compiler_params=small,
        name="combine_one",
    )(got)
    cols = far(near(own))
    sum_spec = pl.BlockSpec((1, PAIR, BLK), lambda i: (i, 0, 0))
    near_sum = pl.pallas_call(
        product_near,
        grid=(Y,),
        in_specs=[held] * (1 + len(NEAR)),
        out_specs=sum_spec,
        out_shape=sum_shape,
        scratch_shapes=[near_stack],
        compiler_params=big,
        cost_estimate=work(len(NEAR), False),
        name="product_near",
    )(near_kernels, *[cols[z] for z in NEAR])
    partial = pl.pallas_call(
        product_far,
        grid=(Y,),
        in_specs=[held, sum_spec] + [held] * Z,
        out_specs=pl.BlockSpec((1, MSG, BLK), lambda i: (i, 0, 0)),
        out_shape=msg_shape,
        scratch_shapes=[far_stack, pltpu.VMEM((EXTRA, BLK), BF16)],
        compiler_params=big,
        cost_estimate=work(len(FAR), False),
        name="product_far",
    )(far_kernels, near_sum, *[cols[z] for z in FAR], *[cols[z] for z in NEAR])
    got = exchange(partial, "row_1")
    scaled, own, to_xy = pl.pallas_call(
        lambda *refs: second_combine(*refs, images=images),
        out_shape=[
            jax.ShapeDtypeStruct(own_shape, F32),
            own_type,
            jax.ShapeDtypeStruct((X * Y, MSG, BLK), BF16),
        ],
        compiler_params=small,
        name="combine_two",
    )(got, inverse)
    last_rows = exchange(to_xy, ("freq", "row_1"))
    partner = lax.ppermute(own, "col", [(0, 1), (1, 0)])
    cols = last_columns(jnp.concatenate([own, partner], axis=0))
    sums = pl.pallas_call(
        sums_kernel,
        grid=(1,),
        in_specs=[pl.BlockSpec((X * Y, EXTRA, BLK), lambda i: (0, PAIR // EXTRA, 0))],
        out_specs=pl.BlockSpec((2 * Z, 8, BLK), lambda i: (0, 0, 0)),
        out_shape=jax.ShapeDtypeStruct((2 * Z, 8, BLK), F32),
        compiler_params=small,
        name="sums",
    )(last_rows)
    sums = exchange(sums, ("row_0", "col"))
    sums, cols = lax.optimization_barrier((sums, cols))
    packed = pl.pallas_call(
        pack_kernel,
        in_specs=[pl.BlockSpec(memory_space=pltpu.SMEM)] + [held] * (1 + X),
        out_specs=held,
        out_shape=jax.ShapeDtypeStruct((ROWS + 2 * X * BLK, BLK), BF16),
        compiler_params=small,
        name="pack",
    )(place, last_rows, *cols)
    packed = lax.ppermute(packed, "col", [(0, 1), (1, 0)])
    tiles, vectors = pl.pallas_call(
        lambda *refs: gram_kernel(*refs, images=images, freqs=freq_total),
        grid_spec=pltpu.PrefetchScalarGridSpec(
            num_scalar_prefetch=1,
            grid=(Y,),
            in_specs=[mask_spec] + [held] * (4 + X),
            out_specs=[
                pl.BlockSpec((X, 1, 2, 2, 32, BLK), lambda i, p: (0, i, 0, 0, 0, 0)),
                pl.BlockSpec((FREQ_DEV, BLK, BLK), lambda i, p: (0, 0, 0)),
            ],
            scratch_shapes=[
                mask_rows,
                pltpu.VMEM((2, 8, BLK), F32),
                pltpu.VMEM((2 * X, 2 * PAIR, BLK), BF16),
            ],
        ),
        out_shape=[
            jax.ShapeDtypeStruct((X, Y, 2, 2, 32, BLK), BF16),
            jax.ShapeDtypeStruct((FREQ_DEV, BLK, BLK), BF16),
        ],
        compiler_params=big,
        name="gram",
    )(place, rows, last_rows, sums, scaled, packed, *cols)
    arrived = exchange(tiles.reshape(X * Y, 2, 2, 32, BLK), ("freq", "row_1"))
    arrived, vectors = lax.optimization_barrier((arrived, vectors))
    vectors = jnp.transpose(vectors, (1, 0, 2))
    affinity = pl.pallas_call(
        final_spread,
        grid_spec=pltpu.PrefetchScalarGridSpec(
            num_scalar_prefetch=1,
            grid=(2,),
            in_specs=[pl.BlockSpec((X * Y, 1, 2, 32, BLK), lambda b, p: (0, b, 0, 0, 0))],
            out_specs=pl.BlockSpec((1, Z, Y, 32, BLK), lambda b, p: (b, 0, 0, 0, 0)),
        ),
        out_shape=jax.ShapeDtypeStruct((2, Z, Y, 32, BLK), F32),
        compiler_params=small,
        name="final",
    )(place, arrived)
    return (vectors, affinity.reshape(2, 32, 1, 1, 32, BLK))


def solution(mesh):
    split = Mesh(
        mesh.devices.reshape(mesh.shape["freq"], 8, 4, mesh.shape["col"]),
        ("freq", "row_0", "row_1", "col"),
    )
    placed = (
        P(ROW_COL, "freq", None, None),
        P(),
        P(ROW_COL, "freq", None),
        P(ROW, None, "col", None),
    )
    return jax.shard_map(
        body,
        mesh=split,
        in_specs=placed,
        out_specs=(P(ROW_COL, "freq", None), P(ROW, None, "col", None, "freq", None)),
        check_vma=False,
    )
```
